256 devices in a mesh: orb: 64 (over y, x, z_lo, core), grid: 4 (over z_hi).
Axes of the slice: x: 4, y: 4, z: 8 (z_hi: 4, z_lo: 2; z = z_hi * 2 + z_lo), core: 2. Of those that a mesh axis runs over, the one named last changes fastest.
Arguments:
- ground_orbitals: float32 [256, 81000], P('orb'), may hold values from -6 to 6
- occupation_signs: int32 [256], P('orb'), may hold values from -1 to 1, as said below
- response_orbitals: float32 [256, 81000], P(('orb', 'grid')), may hold values from -1.5 to 1.5
- window_offsets: int32 [256, 2], P(('orb', 'grid')), may hold values from 0 to 3
- ground_density: float32 [81000], replicated, may hold values from 0.5 to 4
Outputs:
- response_action: float32 [256, 81000], P(('orb', 'grid'))
The draws below stay inside these ranges and needn't reach their ends.
Inputs may be any that keep to these rules, and one draw needn't show every extreme that they name: `occupation_signs`: every entry is -1 or +1.
All inputs are finite; a program needn't handle non-finite values.
Results may differ from the reference program's by a relative error of at most 0.0003.
Values sent between devices are 32-bit elements; how exact they have to be, the bound alone decides.
A program may use at most 128 MiB of HBM per device.

```python
import math
import jax
import jax.numpy as jnp
from jax import lax

NX = 30
NY = 45
NZ = 60
CYCLE = 2
G = 81000
NB = 4
NORB = 256
N_ORB = 64


def draw_occupation_signs(key, part):
    return (2 * jax.random.randint(key, (NORB,), 0, 2) - 1).astype(jnp.int32)


def plant(array, rng, low, high):
    dims = array.shape
    spot = [jax.random.randint(jax.random.fold_in(rng, axis), (), 0, dims[axis]) for axis in range(len(dims))]
    array = array.at[tuple(spot)].set(low)
    longest = dims.index(max(dims))
    spot[longest] = (spot[longest] + 1) % dims[longest]
    return array.at[tuple(spot)].set(high)


def block_scale(stream_key, shape, cuts, smallest, largest):
    gain, own = 1.0, jax.random.fold_in(stream_key, 6)
    for axis_at, shards_of in cuts:
        steps = jnp.exp(jax.random.uniform(jax.random.fold_in(own, axis_at), (shards_of,), jnp.float32, smallest / len(cuts), largest / len(cuts)))
        gain = gain * jnp.repeat(steps, shape[axis_at] // shards_of).reshape([-1 if axis == axis_at else 1 for axis in range(len(shape))])
    return gain


def scatter_about(key, shape, deviation, limit, split=(), dtype=jnp.bfloat16):
    result = jax.random.normal(key, shape, jnp.float32) * deviation
    if len(split) > 0:
        result = block_scale(key, shape, split, -0.22, 0.18) * result
    return jnp.clip(result, min=-limit, max=limit).astype(dtype)


def setup_inputs(seed: int = 0) -> dict:
    key_list = jax.random.split(jax.random.key(seed), 6)
    ground_orbitals = scatter_about(key_list[0], (NORB, G), 1.0, 6.0, ((0, 64),), jnp.float32)
    occupation_signs = draw_occupation_signs(jax.random.fold_in(key_list[5], 71), 0)
    response_orbitals = scatter_about(key_list[2], (NORB, G), 0.25, 1.5, ((0, 256),), jnp.float32)
    window_offsets = plant(jax.random.randint(key_list[3], (NORB, CYCLE), 0, NB), jax.random.fold_in(key_list[3], 1), 0, NB - 1).astype(jnp.int32)
    ground_density = jnp.clip(jnp.exp(jax.random.uniform(key_list[4], (G,), jnp.float32, math.log(0.5), math.log(4.0))), 0.5, 4.0)
    return {"ground_orbitals": ground_orbitals, "occupation_signs": occupation_signs, "response_orbitals": response_orbitals, "window_offsets": window_offsets, "ground_density": ground_density}


SPACING = 0.5
SCREEN = 0.5
XC_COEF = 0.3282
HYBRID = 0.25


def wave_numbers(count):
    positions = jnp.arange(count)
    folded = jnp.where(positions <= count // 2, positions, positions - count)
    return folded.astype(jnp.float32) * (2.0 * math.pi / (count * SPACING))


def coulomb_kernel():
    wave_x = wave_numbers(NX)
    wave_y = wave_numbers(NY)
    wave_z = wave_numbers(NZ)
    squared = wave_x[:, None, None] ** 2 + wave_y[None, :, None] ** 2 + wave_z[None, None, :] ** 2
    return 4.0 * math.pi / (squared + SCREEN * SCREEN)


def poisson(pair, kernel):
    return jnp.real(jnp.fft.ifftn(jnp.fft.fftn(pair) * kernel))


def reference(ground_orbitals, occupation_signs, response_orbitals, window_offsets, ground_density):
    kernel = coulomb_kernel()
    signs = occupation_signs.astype(jnp.float32)
    block_ids = jnp.arange(NB).astype(jnp.int32)

    def single_orbital(orbital):
        response = response_orbitals[orbital].reshape(NX, NY, NZ)
        block_index = orbital // NB

        def cycle_turn(total, cycle_step):
            source = (block_index - cycle_step) % N_ORB
            start = (source * NB).astype(jnp.int32)
            phis = lax.dynamic_slice_in_dim(ground_orbitals, start, NB, 0).reshape(NB, NX, NY, NZ)
            block_signs = lax.dynamic_slice_in_dim(signs, start, NB, 0)
            keep = (block_ids >= window_offsets[orbital, cycle_step]).astype(jnp.float32)
            potentials = jax.vmap(poisson, (0, None))(phis * response[None], kernel)
            weight = (block_signs * keep)[:, None, None, None]
            return total + jnp.sum(weight * phis * potentials, 0), None

        total, _ = lax.scan(cycle_turn, jnp.zeros((NX, NY, NZ), jnp.float32), jnp.arange(CYCLE).astype(jnp.int32))
        return total.reshape(NX * NY * NZ)

    exchange = lax.map(single_orbital, jnp.arange(NORB).astype(jnp.int32))
    density = jnp.sum(signs[:, None] * ground_orbitals * response_orbitals, 0)
    potential = (-XC_COEF * ground_density ** (-2.0 / 3.0)) * density
    return potential[None, :] * ground_orbitals - HYBRID * exchange
```

```python
import math
import numpy as np
import ml_dtypes
import jax
import jax.numpy as jnp
from jax import lax
from jax.experimental import pallas as pl
from jax.experimental.pallas import tpu as pltpu
from jax.sharding import PartitionSpec as P

NX, NY, NZ = 30, 45, 60
NB = 4
YP, ZP = 48, 64
XH = NX // 2
XC_COEF = 0.3282
HYBRID = 0.25


def real_basis(n):
    j = np.arange(n)
    rows, waves = [np.ones(n) / math.sqrt(n)], [0]
    for m in range(1, (n - 1) // 2 + 1):
        rows += [math.sqrt(2 / n) * np.cos(2 * np.pi * m * j / n), math.sqrt(2 / n) * np.sin(2 * np.pi * m * j / n)]
        waves += [m, m]
    if n % 2 == 0:
        rows.append(np.cos(np.pi * j) / math.sqrt(n))
        waves.append(n // 2)
    return np.array(rows), np.array(waves)


def padded(matrix, size):
    return np.pad(matrix, ((0, size - matrix.shape[0]), (0, size - matrix.shape[1])))


def hi_lo(matrix):
    hi = matrix.astype(ml_dtypes.bfloat16)
    lo = (matrix - hi.astype(np.float64)).astype(ml_dtypes.bfloat16)
    return np.stack([hi, lo])


def tables():
    ty, my = real_basis(NY)
    tz, mz = real_basis(NZ)
    ty, tz = padded(ty, YP), padded(tz, ZP)
    wy = np.kron(np.eye(5), ty)
    wz = np.kron(np.eye(NB), tz.T)
    y_mats = np.stack([hi_lo(wy), hi_lo(wy.T)])
    z_mats = np.stack([hi_lo(wz), hi_lo(wz.T)])
    mx = np.arange(NX // 2 + 1)
    k2 = lambda m, n: (2 * np.pi * m / (0.5 * n)) ** 2
    squared = k2(mx, NX)[:, None, None] + k2(my, NY)[None, :, None] + k2(mz, NZ)[None, None, :]
    green = 4 * np.pi / (squared + 0.25)
    weight = np.where((mx == 0) | (mx == NX // 2), 1.0, 2.0) / NX
    green = green * weight[:, None, None]
    green = np.pad(green, ((0, 0), (0, YP - NY), (0, ZP - NZ)))
    green = np.concatenate([green, green], -1).astype(np.float32)
    return y_mats, z_mats, green


def split(x):
    hi = x.astype(jnp.bfloat16)
    return hi, (x - hi.astype(jnp.float32)).astype(jnp.bfloat16)


def dot(a, b):
    return lax.dot_general(a, b, (((1,), (0,)), ((), ())), preferred_element_type=jnp.float32)


def times_right(x, mat):
    hi, lo = split(x)
    return dot(hi, mat[0]) + dot(lo, mat[0]) + dot(hi, mat[1])


def times_left(mat, x):
    hi, lo = split(x)
    return dot(mat[0], hi) + dot(mat[0], lo) + dot(mat[1], hi)


def combine(values, factors):
    total = None
    for value, factor in zip(values, factors):
        if abs(factor) < 1e-12:
            continue
        term = value if factor == 1.0 else (-value if factor == -1.0 else value * factor)
        total = term if total is None else total + term
    return total


def cos_(m, j):
    return round(math.cos(math.pi * ((m * j) % 30) / 15), 15)


def sin_(m, j):
    return round(math.sin(math.pi * ((m * j) % 30) / 15), 15)


EVEN, ODD = range(0, 16, 2), range(1, 16, 2)
EVEN_S, ODD_S = range(2, 15, 2), range(1, 14, 2)


def x_solve(p, green):
    e = [p[0]] + [p[j] + p[NX - j] for j in range(1, 15)] + [p[15]]
    o = [None] + [p[j] - p[NX - j] for j in range(1, 15)]
    a = [e[j] + e[15 - j] for j in range(8)]
    b = [e[j] - e[15 - j] for j in range(8)]
    u = [o[j] + o[15 - j] for j in range(1, 8)]
    w = [o[j] - o[15 - j] for j in range(1, 8)]
    ev = {m: combine(a, [cos_(m, j) for j in range(8)]) * green[m] for m in EVEN}
    od = {m: combine(b, [cos_(m, j) for j in range(8)]) * green[m] for m in ODD}
    so = {m: combine(u, [sin_(m, j) for j in range(1, 8)]) * green[m] for m in ODD_S}
    se = {m: combine(w, [sin_(m, j) for j in range(1, 8)]) * green[m] for m in EVEN_S}
    pe = [combine([ev[m] for m in EVEN], [cos_(m, j) for m in EVEN]) for j in range(8)]
    po = [combine([od[m] for m in ODD], [cos_(m, j) for m in ODD]) for j in range(8)]
    su = [combine([so[m] for m in ODD_S], [sin_(m, j) for m in ODD_S]) for j in range(1, 8)]
    sw = [combine([se[m] for m in EVEN_S], [sin_(m, j) for m in EVEN_S]) for j in range(1, 8)]
    even = [None] * 16
    odd = [None] * 16
    for j in range(8):
        even[j], even[15 - j] = pe[j] + po[j], pe[j] - po[j]
    for j in range(1, 8):
        odd[j], odd[15 - j] = su[j - 1] + sw[j - 1], su[j - 1] - sw[j - 1]
    out = [None] * NX
    out[0], out[15] = even[0], even[15]
    for j in range(1, 15):
        out[j], out[NX - j] = even[j] + odd[j], even[j] - odd[j]
    return out


def forward_yz(t, p_buf, g_buf, d_buf, y_ref, z_ref):
    planes = pl.ds(5 * t, 5)
    p = p_buf[planes].reshape(5 * YP, 128)
    turned = pltpu.roll(p, ZP, 1)
    low = lax.broadcasted_iota(jnp.int32, p.shape, 1) < ZP
    for half in range(2):
        both = jnp.where(low, p, turned) if half == 0 else jnp.where(low, turned, p)
        g = g_buf[half, planes].reshape(5 * YP, 256)
        s = times_right(jnp.concatenate([both, both], 1) * g, z_ref[0])
        d_buf[half, planes] = times_left(y_ref[0], s).reshape(5, YP, 256)


def middle_x(yt, d_buf, green_ref):
    rows = pl.ds(pl.multiple_of(8 * yt, 8), 8)
    green = [green_ref[m, rows, :] for m in range(16)]
    for lane in (0, 128):
        lanes = pl.ds(lane, 128)
        out = x_solve([d_buf[x // XH, x % XH, rows, lanes] for x in range(NX)], green)
        for x in range(NX):
            d_buf[x // XH, x % XH, rows, lanes] = out[x]


def inverse_yz(t, g_buf, d_buf, w, y_ref, z_ref):
    planes = pl.ds(5 * t, 5)
    sums = []
    for half in range(2):
        s = times_left(y_ref[1], d_buf[half, planes].reshape(5 * YP, 256))
        v = times_right(s, z_ref[1]) * (g_buf[half, planes].reshape(5 * YP, 256) * w)
        pair = v[:, :128] + v[:, 128:]
        sums.append(pair + pltpu.roll(pair, ZP, 1))
    low = lax.broadcasted_iota(jnp.int32, sums[0].shape, 1) < ZP
    return jnp.where(low, sums[0], sums[1]).reshape(5, YP, 128)


MESH = pl.DeviceIdType.MESH
HALF = 80
PART = 5
PLANE = 16
RING = 8


def device(orb, grid):
    return {"orb": orb, "grid": grid}


def remote(src, dst, sends, arrivals, target):
    return pltpu.make_async_remote_copy(
        src_ref=src, dst_ref=dst, send_sem=sends, recv_sem=arrivals, device_id=target, device_id_type=MESH
    )


def place_response(p_ref, p_buf):
    @pl.loop(0, XH)
    def _(i):
        p_buf[i] = jnp.zeros((YP, 128), jnp.float32)
        for half in range(2):
            p_buf[i, 0:NY, ZP * half:ZP * half + NZ] = p_ref[i + XH * half]


def place_ground(g_ref, g_buf):
    @pl.loop(0, XH)
    def _(i):
        for half in range(2):
            g_buf[half, i] = jnp.zeros((YP, 256), jnp.float32)
            for q in range(NB):
                g_buf[half, i, 0:NY, ZP * q:ZP * q + NZ] = g_ref[q, i + XH * half]


def kernel(
    g_ref, p_ref, term_ref, signs_ref, offsets_ref, y_ref, z_ref, green_ref,
    e_ref, rho_ref,
    g_buf, p_buf, q_buf, d_own, d_far, e_out, e_in, pair_in, half_sum, plane_in, part_sum, ring_in, part_all,
    p_sems, e_send, e_recv, pair_sems, swap_sems, plane_send, plane_recv, ring_send, ring_recv, all_send, all_recv,
):
    orb, grid = lax.axis_index("orb"), lax.axis_index("grid")
    core = lax.rem(orb, 2)
    z_lo = lax.rem(orb // 2, 2)
    spot = orb // 4
    level = grid * 2 + z_lo
    left = device(lax.rem(orb + 63, 64), grid)
    right = device(lax.rem(orb + 1, 64), grid)
    partner = device(orb + 1 - 2 * core, grid)

    def in_plane(d):
        other = lax.rem(spot + d, PLANE)
        return other, device(other * 4 + lax.rem(orb, 4), grid)

    def in_ring(d):
        other = lax.rem(level + d, RING)
        return device(spot * 4 + lax.rem(other, 2) * 2 + core, other // 2)

    barrier = pltpu.get_barrier_semaphore()

    def greet(target):
        pl.semaphore_signal(barrier, inc=1, device_id=target, device_id_type=MESH)

    for target in (left, right, partner):
        greet(target)

    @pl.loop(1, PLANE)
    def _(d):
        greet(in_plane(d)[1])

    @pl.loop(1, RING)
    def _(d):
        greet(in_ring(d))

    place_response(p_ref, p_buf)
    p_buf[0, NY:YP, :] = jnp.broadcast_to(offsets_ref[1:2, :], (YP - NY, 128))
    pl.semaphore_wait(barrier, 3 + PLANE - 1 + RING - 1)

    give_p = remote(p_buf, q_buf, p_sems.at[0], p_sems.at[1], left)
    give_p.start()
    give_half = remote(term_ref.at[pl.ds((1 - core) * HALF, HALF)], pair_in, pair_sems.at[0], pair_sems.at[1], partner)
    give_half.start()
    place_ground(g_ref, g_buf)
    give_half.wait()
    half_sum[...] = term_ref[pl.ds(core * HALF, HALF)] + pair_in[...]

    def plane_copy(d):
        other, target = in_plane(d)
        return remote(half_sum.at[pl.ds(other * PART, PART)], plane_in.at[d - 1], plane_send.at[d - 1], plane_recv.at[d - 1], target)

    @pl.loop(1, PLANE)
    def _(d):
        plane_copy(d).start()

    signs = signs_ref[...]
    lane_q = (lax.broadcasted_iota(jnp.int32, (1, 256), 1) // ZP).astype(jnp.float32)

    @pl.loop(0, 3)
    def _(t):
        forward_yz(t, p_buf, g_buf, d_own, y_ref, z_ref)

    @pl.loop(1, PLANE)
    def _(d):
        plane_copy(d).wait()

    part = half_sum[pl.ds(spot * PART, PART)]
    for d in range(PLANE - 1):
        part = part + plane_in[d]
    part_sum[...] = part

    def ring_copy(d):
        return remote(part_sum, ring_in.at[d - 1], ring_send.at[d - 1], ring_recv.at[d - 1], in_ring(d))

    @pl.loop(1, RING)
    def _(d):
        ring_copy(d).start()

    give_p.wait_recv()

    @pl.loop(0, 3)
    def _(t):
        forward_yz(t, q_buf, g_buf, d_far, y_ref, z_ref)

    @pl.loop(1, RING)
    def _(d):
        ring_copy(d).wait()

    part = part_sum[...]
    for d in range(RING - 1):
        part = part + ring_in[d]
    part_all[...] = part
    mine = pl.ds(core * HALF + spot * PART, PART)
    rho_ref[mine] = part

    def all_copy(d):
        return remote(part_all, rho_ref.at[mine], all_send.at[d - 1], all_recv.at[d - 1], in_plane(d)[1])

    @pl.loop(1, PLANE)
    def _(d):
        all_copy(d).start()

    @pl.loop(0, YP // 8)
    def _(yt):
        middle_x(yt, d_far, green_ref)

    @pl.loop(1, PLANE)
    def _(d):
        all_copy(d).wait()

    our_half = rho_ref.at[pl.ds(core * HALF, HALF)]
    swap = remote(our_half, our_half, swap_sems.at[0], swap_sems.at[1], partner)
    swap.start()

    far_offset = q_buf[0, NY:NY + 1, :]
    far_w = signs * (lane_q >= jnp.concatenate([far_offset, far_offset], 1)).astype(jnp.float32)
    own_offset = offsets_ref[0:1, :]
    own_w = signs * (lane_q >= jnp.concatenate([own_offset, own_offset], 1)).astype(jnp.float32)

    def e_copy(t):
        planes = pl.ds(5 * t, 5)
        return remote(e_out.at[planes], e_in.at[planes], e_send.at[t], e_recv.at[t], right)

    @pl.loop(0, 3)
    def _(t):
        e_out[pl.ds(5 * t, 5)] = inverse_yz(t, g_buf, d_far, far_w, y_ref, z_ref)
        e_copy(t).start()

    @pl.loop(0, YP // 8)
    def _(yt):
        middle_x(yt, d_own, green_ref)

    @pl.loop(0, 3)
    def _(t):
        own = inverse_yz(t, g_buf, d_own, own_w, y_ref, z_ref)
        e_copy(t).wait()
        own = own + e_in[pl.ds(5 * t, 5)]
        for i in range(5):
            e_ref[5 * t + i] = own[i, :NY, :NZ]
            e_ref[XH + 5 * t + i] = own[i, :NY, ZP:ZP + NZ]

    give_p.wait_send()
    swap.wait()


def per_device(ground_orbitals, occupation_signs, response_orbitals, window_offsets, ground_density):
    points = response_orbitals.shape[1]
    signs = occupation_signs.astype(jnp.float32)
    own_start = lax.axis_index("grid")
    own_ground = lax.dynamic_slice_in_dim(ground_orbitals, own_start, 1, 0).reshape(points)
    own_sign = lax.dynamic_slice_in_dim(signs, own_start, 1, 0)
    response = response_orbitals.reshape(points)
    term = own_sign * own_ground * response
    term = jnp.pad(term, (0, 2 * HALF * 512 - points)).reshape(2 * HALF, 4, 128)
    signs_lanes = jnp.repeat(signs, ZP)[None]
    offsets = jnp.broadcast_to(window_offsets.astype(jnp.float32).reshape(2, 1), (2, 128))
    y_mats, z_mats, green = tables()
    vmem = pl.BlockSpec(memory_space=pltpu.VMEM)
    f32 = jnp.float32
    dma = pltpu.SemaphoreType.DMA
    exchange, rho = pl.pallas_call(
        kernel,
        out_shape=(
            jax.ShapeDtypeStruct((NX, NY, NZ), f32),
            jax.ShapeDtypeStruct((2 * HALF, 4, 128), f32),
        ),
        in_specs=[vmem] * 8,
        out_specs=(vmem, vmem),
        scratch_shapes=[
            pltpu.VMEM((2, XH, YP, 256), f32),
            pltpu.VMEM((XH, YP, 128), f32),
            pltpu.VMEM((XH, YP, 128), f32),
            pltpu.VMEM((2, XH, YP, 256), f32),
            pltpu.VMEM((2, XH, YP, 256), f32),
            pltpu.VMEM((XH, YP, 128), f32),
            pltpu.VMEM((XH, YP, 128), f32),
            pltpu.VMEM((HALF, 4, 128), f32),
            pltpu.VMEM((HALF, 4, 128), f32),
            pltpu.VMEM((PLANE - 1, PART, 4, 128), f32),
            pltpu.VMEM((PART, 4, 128), f32),
            pltpu.VMEM((RING - 1, PART, 4, 128), f32),
            pltpu.VMEM((PART, 4, 128), f32),
            dma((2,)), dma((3,)), dma((3,)), dma((2,)), dma((2,)),
            dma((PLANE - 1,)), dma((PLANE - 1,)), dma((RING - 1,)), dma((RING - 1,)), dma((PLANE - 1,)), dma((PLANE - 1,)),
        ],
        compiler_params=pltpu.CompilerParams(
            collective_id=0, has_side_effects=True, vmem_limit_bytes=48 << 20
        ),
    )(
        ground_orbitals.reshape(NB, NX, NY, NZ), response.reshape(NX, NY, NZ),
        term, signs_lanes, offsets, y_mats, z_mats, green,
    )
    potential = -XC_COEF * ground_density ** (-2.0 / 3.0) * rho.reshape(-1)[:points]
    return (potential * own_ground - HYBRID * exchange.reshape(points))[None]


def solution(mesh):
    placed = (P("orb", None), P("orb"), P(("orb", "grid"), None), P(("orb", "grid"), None), P())
    return jax.shard_map(
        per_device, mesh=mesh, in_specs=placed, out_specs=P(("orb", "grid"), None), check_vma=False
    )
```

```python
import math
import numpy as np
import ml_dtypes
import jax
import jax.numpy as jnp
from jax import lax
from jax.experimental import pallas as pl
from jax.experimental.pallas import tpu as pltpu
from jax.sharding import PartitionSpec as P

NX, NY, NZ = 30, 45, 60
NB = 4
YP, ZP = 48, 64
XH = NX // 2
XC_COEF = 0.3282
HYBRID = 0.25


def real_basis(n):
    j = np.arange(n)
    rows, waves = [np.ones(n) / math.sqrt(n)], [0]
    for m in range(1, (n - 1) // 2 + 1):
        rows += [math.sqrt(2 / n) * np.cos(2 * np.pi * m * j / n), math.sqrt(2 / n) * np.sin(2 * np.pi * m * j / n)]
        waves += [m, m]
    if n % 2 == 0:
        rows.append(np.cos(np.pi * j) / math.sqrt(n))
        waves.append(n // 2)
    return np.array(rows), np.array(waves)


def padded(matrix, size):
    return np.pad(matrix, ((0, size - matrix.shape[0]), (0, size - matrix.shape[1])))


def hi_lo(matrix):
    hi = matrix.astype(ml_dtypes.bfloat16)
    lo = (matrix - hi.astype(np.float64)).astype(ml_dtypes.bfloat16)
    return np.stack([hi, lo])


def tables():
    ty, my = real_basis(NY)
    tz, mz = real_basis(NZ)
    ty, tz = padded(ty, YP), padded(tz, ZP)
    wy = np.kron(np.eye(5), ty)
    wz = np.kron(np.eye(NB), tz.T)
    y_mats = np.stack([hi_lo(wy), hi_lo(wy.T)])
    z_mats = np.stack([hi_lo(wz), hi_lo(wz.T)])
    mx = np.arange(NX // 2 + 1)
    k2 = lambda m, n: (2 * np.pi * m / (0.5 * n)) ** 2
    squared = k2(mx, NX)[:, None, None] + k2(my, NY)[None, :, None] + k2(mz, NZ)[None, None, :]
    green = 4 * np.pi / (squared + 0.25)
    weight = np.where((mx == 0) | (mx == NX // 2), 1.0, 2.0) / NX
    green = green * weight[:, None, None]
    green = np.pad(green, ((0, 0), (0, YP - NY), (0, ZP - NZ)))
    green = np.concatenate([green, green], -1).astype(np.float32)
    return y_mats, z_mats, green


def split(x):
    hi = x.astype(jnp.bfloat16)
    return hi, (x - hi.astype(jnp.float32)).astype(jnp.bfloat16)


def dot(a, b):
    return lax.dot_general(a, b, (((1,), (0,)), ((), ())), preferred_element_type=jnp.float32)


def times_right(x, mat):
    hi, lo = split(x)
    return dot(hi, mat[0]) + dot(lo, mat[0]) + dot(hi, mat[1])


def times_left(mat, x):
    hi, lo = split(x)
    return dot(mat[0], hi) + dot(mat[0], lo) + dot(mat[1], hi)


C3, S3 = 0.5, math.sqrt(3) / 2
S5A, S5B, R5 = math.sin(2 * math.pi / 5), math.sin(4 * math.pi / 5), math.sqrt(5) / 4


def five_even(zero, one, two):
    total, apart = one + two, (one - two) * R5
    base = zero - total * 0.25
    return zero + total, base + apart, base - apart


def five_odd(one, two):
    return one * S5A + two * S5B, one * S5B - two * S5A


def five_waves(p):
    return five_even(p[0], p[1] + p[4], p[2] + p[3]) + five_odd(p[1] - p[4], p[2] - p[3])


def five_points(c):
    zero, one, two = five_even(*c[:3])
    up, down = five_odd(*c[3:])
    return [zero, one + up, two + down, two - down, one - up]


def wave_of(two, three, five):
    wave = next(m for m in range(NX) if (m % 2, m % 3, m % 5) == (two, three, five % 5))
    return min(wave, NX - wave)


def x_solve(p, green):
    grid = [[[p[(15 * a + 10 * b + 6 * c) % NX] for c in range(5)] for b in range(3)] for a in range(2)]
    back = []
    for two in range(2):
        rows = [[grid[0][b][c] - grid[1][b][c] if two else grid[0][b][c] + grid[1][b][c] for c in range(5)] for b in range(3)]
        both = [rows[1][c] + rows[2][c] for c in range(5)]
        flat = five_waves([rows[0][c] + both[c] for c in range(5)])
        cosine = five_waves([rows[0][c] - both[c] * C3 for c in range(5)])
        sine = five_waves([(rows[1][c] - rows[2][c]) * S3 for c in range(5)])
        k = lambda three, five: green[wave_of(two, three, five)]
        flat = [flat[0] * k(0, 0), flat[1] * k(0, 1), flat[2] * k(0, 2), flat[3] * k(0, 1), flat[4] * k(0, 2)]
        new_c, new_s = [cosine[0] * k(1, 0)] + [None] * 4, [sine[0] * k(1, 0)] + [None] * 4
        for five in (1, 2):
            cc, cs, sc, ss = cosine[five], cosine[five + 2], sine[five], sine[five + 2]
            x_up, x_down = (cc - ss) * k(1, five), (cc + ss) * k(1, -five)
            y_up, y_down = (sc + cs) * k(1, five), (sc - cs) * k(1, -five)
            new_c[five], new_s[five + 2] = x_up + x_down, x_down - x_up
            new_s[five], new_c[five + 2] = y_up + y_down, y_up - y_down
        flat, cosine, sine = five_points(flat), five_points(new_c), five_points(new_s)
        lines = [[flat[c] + cosine[c] for c in range(5)], [], []]
        for c in range(5):
            middle, side = flat[c] - cosine[c] * C3, sine[c] * S3
            lines[1].append(middle + side)
            lines[2].append(middle - side)
        back.append(lines)
    out = [None] * NX
    for a in range(2):
        for b in range(3):
            for c in range(5):
                plus, minus = back[0][b][c], back[1][b][c]
                out[(15 * a + 10 * b + 6 * c) % NX] = minus_or(plus, minus, a)
    return out


def minus_or(plus, minus, a):
    return plus - minus if a else plus + minus


def forward_yz(t, p_buf, g_buf, d_buf, y_ref, z_ref):
    planes = pl.ds(5 * t, 5)
    p = p_buf[planes].reshape(5 * YP, 128)
    turned = pltpu.roll(p, ZP, 1)
    low = lax.broadcasted_iota(jnp.int32, p.shape, 1) < ZP
    for half in range(2):
        both = jnp.where(low, p, turned) if half == 0 else jnp.where(low, turned, p)
        g = g_buf[half, planes].reshape(5 * YP, 256)
        s = times_right(jnp.concatenate([both, both], 1) * g, z_ref[0])
        d_buf[half, planes] = times_left(y_ref[0], s).reshape(5, YP, 256)


def middle_x(yt, d_buf, green_ref):
    rows = pl.ds(pl.multiple_of(8 * yt, 8), 8)
    green = [green_ref[m, rows, :] for m in range(16)]
    for lane in (0, 128):
        lanes = pl.ds(lane, 128)
        out = x_solve([d_buf[x // XH, x % XH, rows, lanes] for x in range(NX)], green)
        for x in range(NX):
            d_buf[x // XH, x % XH, rows, lanes] = out[x]


def inverse_yz(t, g_buf, d_buf, w, y_ref, z_ref):
    planes = pl.ds(5 * t, 5)
    sums = []
    for half in range(2):
        s = times_left(y_ref[1], d_buf[half, planes].reshape(5 * YP, 256))
        v = times_right(s, z_ref[1]) * (g_buf[half, planes].reshape(5 * YP, 256) * w)
        pair = v[:, :128] + v[:, 128:]
        sums.append(pair + pltpu.roll(pair, ZP, 1))
    low = lax.broadcasted_iota(jnp.int32, sums[0].shape, 1) < ZP
    return jnp.where(low, sums[0], sums[1]).reshape(5, YP, 128)


MESH = pl.DeviceIdType.MESH
HALF = 80
PART = 5
PLANE = 16
RING = 8


def device(orb, grid):
    return {"orb": orb, "grid": grid}


def remote(src, dst, sends, arrivals, target):
    return pltpu.make_async_remote_copy(
        src_ref=src, dst_ref=dst, send_sem=sends, recv_sem=arrivals, device_id=target, device_id_type=MESH
    )


def drain(ref, sem):
    pltpu.make_async_copy(ref, ref, sem).wait()


def place_response(p_ref, p_buf):
    @pl.loop(0, XH)
    def _(i):
        p_buf[i] = jnp.zeros((YP, 128), jnp.float32)
        for half in range(2):
            p_buf[i, 0:NY, ZP * half:ZP * half + NZ] = p_ref[i + XH * half]


def place_ground(g_ref, g_buf):
    @pl.loop(0, XH)
    def _(i):
        for half in range(2):
            g_buf[half, i] = jnp.zeros((YP, 256), jnp.float32)
            for q in range(NB):
                g_buf[half, i, 0:NY, ZP * q:ZP * q + NZ] = g_ref[q, i + XH * half]


def kernel(
    g_ref, p_ref, term_ref, signs_ref, offsets_ref, y_ref, z_ref, green_ref,
    e_ref, rho_ref,
    g_buf, p_buf, q_buf, d_own, d_far, e_out, e_in, pair_in, half_sum, plane_in, part_sum, ring_in, part_all,
    p_sems, e_send, e_recv, pair_sems, swap_sems, plane_send, plane_recv, ring_send, ring_recv, all_send, all_recv,
):
    orb, grid = lax.axis_index("orb"), lax.axis_index("grid")
    core = lax.rem(orb, 2)
    z_lo = lax.rem(orb // 2, 2)
    spot = orb // 4
    level = grid * 2 + z_lo
    left = device(lax.rem(orb + 63, 64), grid)
    right = device(lax.rem(orb + 1, 64), grid)
    partner = device(orb + 1 - 2 * core, grid)

    def in_plane(d):
        other = lax.rem(spot + d, PLANE)
        return other, device(other * 4 + lax.rem(orb, 4), grid)

    def in_ring(d):
        other = lax.rem(level + d, RING)
        return device(spot * 4 + lax.rem(other, 2) * 2 + core, other // 2)

    barrier = pltpu.get_barrier_semaphore()

    def greet(target):
        pl.semaphore_signal(barrier, inc=1, device_id=target, device_id_type=MESH)

    for target in (left, right, partner):
        greet(target)

    @pl.loop(1, PLANE)
    def _(d):
        greet(in_plane(d)[1])

    @pl.loop(1, RING)
    def _(d):
        greet(in_ring(d))

    place_response(p_ref, p_buf)
    p_buf[0, NY:YP, :] = jnp.broadcast_to(offsets_ref[1:2, :], (YP - NY, 128))
    pl.semaphore_wait(barrier, 3 + PLANE - 1 + RING - 1)

    give_p = remote(p_buf, q_buf, p_sems.at[0], p_sems.at[1], left)
    give_p.start()
    give_half = remote(term_ref.at[pl.ds((1 - core) * HALF, HALF)], pair_in, pair_sems.at[0], pair_sems.at[1], partner)
    give_half.start()
    place_ground(g_ref, g_buf)
    give_half.wait()
    half_sum[...] = term_ref[pl.ds(core * HALF, HALF)] + pair_in[...]

    def plane_copy(d):
        other, target = in_plane(d)
        return remote(half_sum.at[pl.ds(other * PART, PART)], plane_in.at[d - 1], plane_send, plane_recv, target)

    @pl.loop(1, PLANE)
    def _(d):
        plane_copy(d).start()

    signs = signs_ref[...]
    lane_q = (lax.broadcasted_iota(jnp.int32, (1, 256), 1) // ZP).astype(jnp.float32)

    for t in range(3):
        forward_yz(t, p_buf, g_buf, d_own, y_ref, z_ref)

    drain(half_sum.at[pl.ds(0, HALF - PART)], plane_send)
    drain(plane_in, plane_recv)

    part = half_sum[pl.ds(spot * PART, PART)]
    for d in range(PLANE - 1):
        part = part + plane_in[d]
    part_sum[...] = part

    def ring_copy(d):
        return remote(part_sum, ring_in.at[d - 1], ring_send, ring_recv, in_ring(d))

    @pl.loop(1, RING)
    def _(d):
        ring_copy(d).start()

    give_p.wait_recv()

    for t in range(3):
        forward_yz(t, q_buf, g_buf, d_far, y_ref, z_ref)

    drain(ring_in, ring_send)
    drain(ring_in, ring_recv)

    part = part_sum[...]
    for d in range(RING - 1):
        part = part + ring_in[d]
    part_all[...] = part
    mine = pl.ds(core * HALF + spot * PART, PART)
    rho_ref[mine] = part

    def all_copy(d):
        return remote(part_all, rho_ref.at[mine], all_send, all_recv, in_plane(d)[1])

    @pl.loop(1, PLANE)
    def _(d):
        all_copy(d).start()

    @pl.loop(0, YP // 8)
    def _(yt):
        middle_x(yt, d_far, green_ref)

    drain(half_sum.at[pl.ds(0, HALF - PART)], all_send)
    drain(half_sum.at[pl.ds(0, HALF - PART)], all_recv)

    our_half = rho_ref.at[pl.ds(core * HALF, HALF)]
    swap = remote(our_half, our_half, swap_sems.at[0], swap_sems.at[1], partner)
    swap.start()

    far_offset = q_buf[0, NY:NY + 1, :]
    far_w = signs * (lane_q >= jnp.concatenate([far_offset, far_offset], 1)).astype(jnp.float32)
    own_offset = offsets_ref[0:1, :]
    own_w = signs * (lane_q >= jnp.concatenate([own_offset, own_offset], 1)).astype(jnp.float32)

    def e_copy(t):
        planes = pl.ds(5 * t, 5)
        return remote(e_out.at[planes], e_in.at[planes], e_send.at[t], e_recv.at[t], right)

    for t in range(3):
        e_out[pl.ds(5 * t, 5)] = inverse_yz(t, g_buf, d_far, far_w, y_ref, z_ref)
        e_copy(t).start()

    @pl.loop(0, YP // 8)
    def _(yt):
        middle_x(yt, d_own, green_ref)

    for t in range(3):
        own = inverse_yz(t, g_buf, d_own, own_w, y_ref, z_ref)
        e_copy(t).wait()
        own = own + e_in[pl.ds(5 * t, 5)]
        for i in range(5):
            e_ref[5 * t + i] = own[i, :NY, :NZ]
            e_ref[XH + 5 * t + i] = own[i, :NY, ZP:ZP + NZ]

    give_p.wait_send()
    swap.wait()


def per_device(ground_orbitals, occupation_signs, response_orbitals, window_offsets, ground_density):
    points = response_orbitals.shape[1]
    signs = occupation_signs.astype(jnp.float32)
    own_start = lax.axis_index("grid")
    own_ground = lax.dynamic_slice_in_dim(ground_orbitals, own_start, 1, 0).reshape(points)
    own_sign = lax.dynamic_slice_in_dim(signs, own_start, 1, 0)
    response = response_orbitals.reshape(points)
    term = own_sign * own_ground * response
    term = jnp.pad(term, (0, 2 * HALF * 512 - points)).reshape(2 * HALF, 4, 128)
    signs_lanes = jnp.repeat(signs, ZP)[None]
    offsets = jnp.broadcast_to(window_offsets.astype(jnp.float32).reshape(2, 1), (2, 128))
    y_mats, z_mats, green = tables()
    vmem = pl.BlockSpec(memory_space=pltpu.VMEM)
    f32 = jnp.float32
    dma = pltpu.SemaphoreType.DMA
    exchange, rho = pl.pallas_call(
        kernel,
        out_shape=(
            jax.ShapeDtypeStruct((NX, NY, NZ), f32),
            jax.ShapeDtypeStruct((2 * HALF, 4, 128), f32),
        ),
        in_specs=[vmem] * 8,
        out_specs=(vmem, vmem),
        scratch_shapes=[
            pltpu.VMEM((2, XH, YP, 256), f32),
            pltpu.VMEM((XH, YP, 128), f32),
            pltpu.VMEM((XH, YP, 128), f32),
            pltpu.VMEM((2, XH, YP, 256), f32),
            pltpu.VMEM((2, XH, YP, 256), f32),
            pltpu.VMEM((XH, YP, 128), f32),
            pltpu.VMEM((XH, YP, 128), f32),
            pltpu.VMEM((HALF, 4, 128), f32),
            pltpu.VMEM((HALF, 4, 128), f32),
            pltpu.VMEM((PLANE - 1, PART, 4, 128), f32),
            pltpu.VMEM((PART, 4, 128), f32),
            pltpu.VMEM((RING - 1, PART, 4, 128), f32),
            pltpu.VMEM((PART, 4, 128), f32),
            dma((2,)), dma((3,)), dma((3,)), dma((2,)), dma((2,)),
            dma, dma, dma, dma, dma, dma,
        ],
        compiler_params=pltpu.CompilerParams(
            collective_id=0, has_side_effects=True, vmem_limit_bytes=48 << 20
        ),
    )(
        ground_orbitals.reshape(NB, NX, NY, NZ), response.reshape(NX, NY, NZ),
        term, signs_lanes, offsets, y_mats, z_mats, green,
    )
    potential = -XC_COEF * ground_density ** (-2.0 / 3.0) * rho.reshape(-1)[:points]
    return (potential * own_ground - HYBRID * exchange.reshape(points))[None]


def solution(mesh):
    placed = (P("orb", None), P("orb"), P(("orb", "grid"), None), P(("orb", "grid"), None), P())
    return jax.shard_map(
        per_device, mesh=mesh, in_specs=placed, out_specs=P(("orb", "grid"), None), check_vma=False
    )
```

```python
import math
import numpy as np
import ml_dtypes
import jax
import jax.numpy as jnp
from jax import lax
from jax.experimental import pallas as pl
from jax.experimental.pallas import tpu as pltpu
from jax.sharding import PartitionSpec as P

NX, NY, NZ = 30, 45, 60
NB = 4
YP, ZP = 48, 64
XH = NX // 2
XC_COEF = 0.3282
HYBRID = 0.25


def real_basis(n):
    j = np.arange(n)
    rows, waves = [np.ones(n) / math.sqrt(n)], [0]
    for m in range(1, (n - 1) // 2 + 1):
        rows += [math.sqrt(2 / n) * np.cos(2 * np.pi * m * j / n), math.sqrt(2 / n) * np.sin(2 * np.pi * m * j / n)]
        waves += [m, m]
    if n % 2 == 0:
        rows.append(np.cos(np.pi * j) / math.sqrt(n))
        waves.append(n // 2)
    return np.array(rows), np.array(waves)


def padded(matrix, size):
    return np.pad(matrix, ((0, size - matrix.shape[0]), (0, size - matrix.shape[1])))


def hi_lo(matrix):
    hi = matrix.astype(ml_dtypes.bfloat16)
    lo = (matrix - hi.astype(np.float64)).astype(ml_dtypes.bfloat16)
    return np.stack([hi, lo])


def tables():
    ty, my = real_basis(NY)
    tz, mz = real_basis(NZ)
    ty, tz = padded(ty, YP), padded(tz, ZP)
    wy = np.kron(np.eye(5), ty)
    wz = np.kron(np.eye(NB), tz.T)
    y_mats = np.stack([hi_lo(wy), hi_lo(wy.T)])
    z_mats = np.stack([hi_lo(wz), hi_lo(wz.T)])
    mx = np.arange(NX // 2 + 1)
    k2 = lambda m, n: (2 * np.pi * m / (0.5 * n)) ** 2
    squared = k2(mx, NX)[:, None, None] + k2(my, NY)[None, :, None] + k2(mz, NZ)[None, None, :]
    green = 4 * np.pi / (squared + 0.25)
    weight = np.where((mx == 0) | (mx == NX // 2), 1.0, 2.0) / NX
    green = green * weight[:, None, None]
    green = np.pad(green, ((0, 0), (0, YP - NY), (0, ZP - NZ)))
    green = np.concatenate([green, green], -1).astype(np.float32)
    return y_mats, z_mats, green


def split(x):
    hi = x.astype(jnp.bfloat16)
    return hi, (x - hi.astype(jnp.float32)).astype(jnp.bfloat16)


def dot(a, b):
    return lax.dot_general(a, b, (((1,), (0,)), ((), ())), preferred_element_type=jnp.float32)


def times_right(x, mat):
    hi, lo = split(x)
    return dot(hi, mat[0]) + dot(lo, mat[0]) + dot(hi, mat[1])


def times_left(mat, x):
    hi, lo = split(x)
    return dot(mat[0], hi) + dot(mat[0], lo) + dot(mat[1], hi)


C3, S3 = 0.5, math.sqrt(3) / 2
S5A, S5B, R5 = math.sin(2 * math.pi / 5), math.sin(4 * math.pi / 5), math.sqrt(5) / 4


def five_even(zero, one, two):
    total, apart = one + two, (one - two) * R5
    base = zero - total * 0.25
    return zero + total, base + apart, base - apart


def five_odd(one, two):
    return one * S5A + two * S5B, one * S5B - two * S5A


def five_waves(p):
    return five_even(p[0], p[1] + p[4], p[2] + p[3]) + five_odd(p[1] - p[4], p[2] - p[3])


def five_points(c):
    zero, one, two = five_even(*c[:3])
    up, down = five_odd(*c[3:])
    return [zero, one + up, two + down, two - down, one - up]


def wave_of(two, three, five):
    wave = next(m for m in range(NX) if (m % 2, m % 3, m % 5) == (two, three, five % 5))
    return min(wave, NX - wave)


def x_solve(p, green):
    grid = [[[p[(15 * a + 10 * b + 6 * c) % NX] for c in range(5)] for b in range(3)] for a in range(2)]
    back = []
    for two in range(2):
        rows = [[grid[0][b][c] - grid[1][b][c] if two else grid[0][b][c] + grid[1][b][c] for c in range(5)] for b in range(3)]
        both = [rows[1][c] + rows[2][c] for c in range(5)]
        flat = five_waves([rows[0][c] + both[c] for c in range(5)])
        cosine = five_waves([rows[0][c] - both[c] * C3 for c in range(5)])
        sine = five_waves([(rows[1][c] - rows[2][c]) * S3 for c in range(5)])
        k = lambda three, five: green[wave_of(two, three, five)]
        flat = [flat[0] * k(0, 0), flat[1] * k(0, 1), flat[2] * k(0, 2), flat[3] * k(0, 1), flat[4] * k(0, 2)]
        new_c, new_s = [cosine[0] * k(1, 0)] + [None] * 4, [sine[0] * k(1, 0)] + [None] * 4
        for five in (1, 2):
            cc, cs, sc, ss = cosine[five], cosine[five + 2], sine[five], sine[five + 2]
            x_up, x_down = (cc - ss) * k(1, five), (cc + ss) * k(1, -five)
            y_up, y_down = (sc + cs) * k(1, five), (sc - cs) * k(1, -five)
            new_c[five], new_s[five + 2] = x_up + x_down, x_down - x_up
            new_s[five], new_c[five + 2] = y_up + y_down, y_up - y_down
        flat, cosine, sine = five_points(flat), five_points(new_c), five_points(new_s)
        lines = [[flat[c] + cosine[c] for c in range(5)], [], []]
        for c in range(5):
            middle, side = flat[c] - cosine[c] * C3, sine[c] * S3
            lines[1].append(middle + side)
            lines[2].append(middle - side)
        back.append(lines)
    out = [None] * NX
    for a in range(2):
        for b in range(3):
            for c in range(5):
                plus, minus = back[0][b][c], back[1][b][c]
                out[(15 * a + 10 * b + 6 * c) % NX] = minus_or(plus, minus, a)
    return out


def minus_or(plus, minus, a):
    return plus - minus if a else plus + minus


def forward_yz(t, p_buf, g_buf, d_buf, y_ref, z_ref):
    planes = pl.ds(5 * t, 5)
    p = p_buf[planes].reshape(5 * YP, 128)
    turned = pltpu.roll(p, ZP, 1)
    low = lax.broadcasted_iota(jnp.int32, p.shape, 1) < ZP
    for half in range(2):
        both = jnp.where(low, p, turned) if half == 0 else jnp.where(low, turned, p)
        g = g_buf[half, planes].reshape(5 * YP, 256)
        s = times_right(jnp.concatenate([both, both], 1) * g, z_ref[0])
        d_buf[half, planes] = times_left(y_ref[0], s).reshape(5, YP, 256)


def middle_x(yt, d_buf, green_ref):
    rows = pl.ds(pl.multiple_of(8 * yt, 8), 8)
    green = [green_ref[m, rows, :] for m in range(16)]
    for lane in (0, 128):
        lanes = pl.ds(lane, 128)
        out = x_solve([d_buf[x // XH, x % XH, rows, lanes] for x in range(NX)], green)
        for x in range(NX):
            d_buf[x // XH, x % XH, rows, lanes] = out[x]


def inverse_yz(t, g_buf, d_buf, w, y_ref, z_ref):
    planes = pl.ds(5 * t, 5)
    sums = []
    for half in range(2):
        s = times_left(y_ref[1], d_buf[half, planes].reshape(5 * YP, 256))
        v = times_right(s, z_ref[1]) * (g_buf[half, planes].reshape(5 * YP, 256) * w)
        pair = v[:, :128] + v[:, 128:]
        sums.append(pair + pltpu.roll(pair, ZP, 1))
    low = lax.broadcasted_iota(jnp.int32, sums[0].shape, 1) < ZP
    return jnp.where(low, sums[0], sums[1]).reshape(5, YP, 128)


MESH = pl.DeviceIdType.MESH
SPOTS = 16
CHIPS = 32
RING = 8
ROWS = 24
WINDOW = 1920
TILES = 15


def device(orb, grid):
    return {"orb": orb, "grid": grid}


def remote(src, dst, sends, arrivals, target):
    return pltpu.make_async_remote_copy(
        src_ref=src, dst_ref=dst, send_sem=sends, recv_sem=arrivals, device_id=target, device_id_type=MESH
    )


def drain(ref, sem):
    pltpu.make_async_copy(ref, ref, sem).wait()


def cut_rows(flat, last, rows, points):
    lane = lax.broadcasted_iota(jnp.int32, (8, 128), 1)

    def cut(base, count, tile):
        for r in range(count):
            j, off = divmod(NZ * r, 128)
            both = tile(j) if off <= 128 - NZ else jnp.where(lane < off, tile(j + 1), tile(j))
            rows[pl.ds(base + 8 * r, 8), :] = pltpu.roll(both, 128 - off, 1) if off else both

    whole = points // WINDOW
    tail = points - points // 128 * 128
    last[...] = jnp.zeros((8, 128), jnp.float32)
    last[:, 0:tail] = flat[:, points - tail:points]

    @pl.loop(0, whole, unroll=6)
    def _(k):
        cut(
            pl.multiple_of(k * 256, 256), 32,
            lambda j: flat[:, pl.ds(pl.multiple_of(k * WINDOW + j * 128, 128), 128)],
        )

    end = whole * TILES
    cut(
        whole * 256, (points - whole * WINDOW) // NZ,
        lambda j: last[...] if end + j == points // 128 else flat[:, (end + j) * 128:(end + j + 1) * 128],
    )
    rows[8 * (NX * NY):8 * (NX * NY + YP - NY), :] = jnp.zeros((8 * (YP - NY), 128), jnp.float32)


def plane(rows, x, line):
    return rows[pl.ds(x * (8 * NY) + line, YP, stride=8), :]


def kernel(
    ground_ref, response_ref, density_ref, signs_ref, offsets_ref, y_ref, z_ref, green_ref,
    out_ref,
    flat, last, rows, g_buf, p_buf, q_buf, own_buf, d_own, d_far, e_out, e_in,
    term, pair_in, half_sum, plane_in, part_sum, ring_in, part_all, rho,
    in_sems, p_sems, e_send, e_recv, pair_sems, plane_send, plane_recv, ring_send, ring_recv, all_send, all_recv,
):
    orb, grid = lax.axis_index("orb"), lax.axis_index("grid")
    core = lax.rem(orb, 2)
    z_lo = lax.rem(orb // 2, 2)
    spot = orb // 4
    level = grid * 2 + z_lo
    left = device(lax.rem(orb + 63, 64), grid)
    right = device(lax.rem(orb + 1, 64), grid)
    partner = device(orb + 1 - 2 * core, grid)

    loads = (
        pltpu.make_async_copy(ground_ref, flat.at[0:NB], in_sems.at[0]),
        pltpu.make_async_copy(response_ref, flat.at[NB:NB + 1], in_sems.at[1]),
    )
    for load in loads:
        load.start()

    def in_plane(d):
        other = lax.rem(spot + d, SPOTS)
        return other, device(other * 4 + lax.rem(orb, 4), grid)

    def in_chips(d):
        other = lax.rem(spot * 2 + core + d, CHIPS)
        return device(other // 2 * 4 + z_lo * 2 + lax.rem(other, 2), grid)

    def in_ring(d):
        other = lax.rem(level + d, RING)
        return device(spot * 4 + lax.rem(other, 2) * 2 + core, other // 2)

    barrier = pltpu.get_barrier_semaphore()

    def greet(target):
        pl.semaphore_signal(barrier, inc=1, device_id=target, device_id_type=MESH)

    for target in (left, right):
        greet(target)

    @pl.loop(1, CHIPS)
    def _(d):
        greet(in_chips(d))

    @pl.loop(1, RING)
    def _(d):
        greet(in_ring(d))

    for load in loads:
        load.wait()
    cut_rows(flat, last, rows, flat.shape[1])

    low = lax.broadcasted_iota(jnp.int32, (YP, 128), 1) < ZP
    own_sign = signs_ref[grid].astype(jnp.float32)

    def packed(i, line):
        return jnp.where(low, plane(rows, i, line), pltpu.roll(plane(rows, i + XH, line), ZP, 1))

    @pl.loop(0, XH)
    def _(i):
        p, own = packed(i, NB), packed(i, grid)
        p_buf[i] = p
        own_buf[i] = own
        term[pl.ds(2 * i, 2)] = (own * own_sign * p).reshape(2, ROWS, 128)

    term[2 * XH:CHIPS] = jnp.zeros((CHIPS - 2 * XH, ROWS, 128), jnp.float32)
    p_buf[0, NY:YP, :] = jnp.broadcast_to(offsets_ref[0, 1].astype(jnp.float32), (YP - NY, 128))
    pl.semaphore_wait(barrier, 2 + CHIPS - 1 + RING - 1)

    give_half = remote(term.at[pl.ds((1 - core) * SPOTS, SPOTS)], pair_in, pair_sems.at[0], pair_sems.at[1], partner)
    give_half.start()

    @pl.loop(0, XH)
    def _(i):
        for half in range(2):
            x = i + XH * half
            for pair in (0, 2):
                g = jnp.where(low, plane(rows, x, pair), pltpu.roll(plane(rows, x, pair + 1), ZP, 1))
                g_buf[half, i, :, 64 * pair:64 * pair + 128] = g

    give_half.wait()
    half_sum[...] = term[pl.ds(core * SPOTS, SPOTS)] + pair_in[...]

    @pl.loop(1, SPOTS)
    def _(d):
        other, target = in_plane(d)
        remote(half_sum.at[other], plane_in.at[d - 1], plane_send, plane_recv, target).start()

    give_p = remote(p_buf, q_buf, p_sems.at[0], p_sems.at[1], left)
    give_p.start()

    for t in range(3):
        forward_yz(t, p_buf, g_buf, d_own, y_ref, z_ref)

    drain(half_sum.at[pl.ds(0, SPOTS - 1)], plane_send)
    drain(plane_in, plane_recv)
    part = half_sum[spot]
    for d in range(SPOTS - 1):
        part = part + plane_in[d]
    part_sum[...] = part

    @pl.loop(1, RING)
    def _(d):
        remote(part_sum, ring_in.at[d - 1], ring_send, ring_recv, in_ring(d)).start()

    give_p.wait_recv()

    for t in range(3):
        forward_yz(t, q_buf, g_buf, d_far, y_ref, z_ref)

    drain(ring_in, ring_send)
    drain(ring_in, ring_recv)
    part = part_sum[...]
    for d in range(RING - 1):
        part = part + ring_in[d]
    part_all[...] = part
    mine = core * SPOTS + spot
    rho[mine] = part

    @pl.loop(1, CHIPS)
    def _(d):
        remote(part_all, rho.at[mine], all_send, all_recv, in_chips(d)).start()

    @pl.loop(0, YP // 8)
    def _(yt):
        middle_x(yt, d_far, green_ref)

    lane_q = lax.broadcasted_iota(jnp.int32, (1, 256), 1) // ZP
    signs = jnp.zeros((1, 256), jnp.float32)
    for q in range(NB):
        signs = jnp.where(lane_q == q, signs_ref[q].astype(jnp.float32), signs)
    lane_q = lane_q.astype(jnp.float32)
    far_offset = q_buf[0, NY:NY + 1, :]
    far_w = signs * (lane_q >= jnp.concatenate([far_offset, far_offset], 1)).astype(jnp.float32)
    own_offset = jnp.broadcast_to(offsets_ref[0, 0].astype(jnp.float32), (1, 256))
    own_w = signs * (lane_q >= own_offset).astype(jnp.float32)

    def e_copy(t):
        planes = pl.ds(5 * t, 5)
        return remote(e_out.at[planes], e_in.at[planes], e_send.at[t], e_recv.at[t], right)

    for t in range(3):
        e_out[pl.ds(5 * t, 5)] = inverse_yz(t, g_buf, d_far, far_w, y_ref, z_ref)
        e_copy(t).start()

    @pl.loop(0, XH)
    def _(i):
        for half in range(2):
            p_buf_lanes = pl.ds(ZP * half, NZ)
            density = density_ref[i + XH * half]
            scale = jnp.exp(jnp.log(density) * (-2.0 / 3.0)) * -XC_COEF
            own_buf[i, 0:NY, p_buf_lanes] = own_buf[i, 0:NY, p_buf_lanes] * scale

    @pl.loop(0, YP // 8)
    def _(yt):
        middle_x(yt, d_own, green_ref)

    for t in range(3):
        e_out_t = inverse_yz(t, g_buf, d_own, own_w, y_ref, z_ref)
        e_copy(t).wait()
        e_in[pl.ds(5 * t, 5)] = (e_out_t + e_in[pl.ds(5 * t, 5)]) * -HYBRID

    drain(rho.at[pl.ds(0, CHIPS - 1)], all_send)
    drain(rho.at[pl.ds(0, CHIPS - 1)], all_recv)

    @pl.loop(0, XH)
    def _(i):
        total = own_buf[i] * rho[pl.ds(2 * i, 2)].reshape(YP, 128) + e_in[i]
        out_ref[i] = total[:NY, :NZ]
        out_ref[XH + i] = total[:NY, ZP:ZP + NZ]

    give_p.wait_send()


def per_device(ground_orbitals, occupation_signs, response_orbitals, window_offsets, ground_density):
    points = response_orbitals.shape[1]
    y_mats, z_mats, green = tables()
    vmem = pl.BlockSpec(memory_space=pltpu.VMEM)
    smem = pl.BlockSpec(memory_space=pltpu.SMEM)
    hbm = pl.BlockSpec(memory_space=pltpu.HBM)
    f32 = jnp.float32
    dma = pltpu.SemaphoreType.DMA
    grid_planes = pltpu.VMEM((XH, YP, 128), f32)
    wide_planes = pltpu.VMEM((2, XH, YP, 256), f32)

    def chunks(*count):
        return pltpu.VMEM((*count, ROWS, 128), f32)

    action = pl.pallas_call(
        kernel,
        out_shape=jax.ShapeDtypeStruct((NX, NY, NZ), f32),
        in_specs=[hbm, hbm, vmem, smem, smem, vmem, vmem, vmem],
        out_specs=vmem,
        scratch_shapes=[
            pltpu.VMEM((8, points), f32),
            pltpu.VMEM((8, 128), f32),
            pltpu.VMEM((8 * (NX * NY + YP - NY), 128), f32),
            wide_planes, grid_planes, grid_planes, grid_planes, wide_planes, wide_planes, grid_planes, grid_planes,
            chunks(CHIPS), chunks(SPOTS), chunks(SPOTS), chunks(SPOTS - 1), chunks(), chunks(RING - 1), chunks(), chunks(CHIPS),
            dma((2,)), dma((2,)), dma((3,)), dma((3,)), dma((2,)), dma, dma, dma, dma, dma, dma,
        ],
        compiler_params=pltpu.CompilerParams(
            collective_id=0, has_side_effects=True, vmem_limit_bytes=28 << 20
        ),
    )(
        ground_orbitals, response_orbitals, ground_density.reshape(NX, NY, NZ),
        occupation_signs, window_offsets, y_mats, z_mats, green,
    )
    return action.reshape(1, points)


def solution(mesh):
    placed = (P("orb", None), P("orb"), P(("orb", "grid"), None), P(("orb", "grid"), None), P())
    return jax.shard_map(
        per_device, mesh=mesh, in_specs=placed, out_specs=P(("orb", "grid"), None), check_vma=False
    )
```

```python
import math
import numpy as np
import ml_dtypes
import jax
import jax.numpy as jnp
from jax import lax
from jax.experimental import pallas as pl
from jax.experimental.pallas import tpu as pltpu
from jax.sharding import PartitionSpec as P

NX, NY, NZ = 30, 45, 60
NB = 4
YP, ZP = 48, 64
XH = NX // 2
XC_COEF = 0.3282
HYBRID = 0.25


def real_basis(n):
    j = np.arange(n)
    rows, waves = [np.ones(n) / math.sqrt(n)], [0]
    for m in range(1, (n - 1) // 2 + 1):
        rows += [math.sqrt(2 / n) * np.cos(2 * np.pi * m * j / n), math.sqrt(2 / n) * np.sin(2 * np.pi * m * j / n)]
        waves += [m, m]
    if n % 2 == 0:
        rows.append(np.cos(np.pi * j) / math.sqrt(n))
        waves.append(n // 2)
    return np.array(rows), np.array(waves)


def padded(matrix, size):
    return np.pad(matrix, ((0, size - matrix.shape[0]), (0, size - matrix.shape[1])))


def hi_lo(matrix):
    hi = matrix.astype(ml_dtypes.bfloat16)
    lo = (matrix - hi.astype(np.float64)).astype(ml_dtypes.bfloat16)
    return np.stack([hi, lo])


def tables():
    ty, my = real_basis(NY)
    tz, mz = real_basis(NZ)
    ty, tz = padded(ty, YP), padded(tz, ZP)
    wy = np.kron(np.eye(5), ty)
    wz = np.kron(np.eye(NB), tz.T)
    y_mats = np.stack([hi_lo(wy), hi_lo(wy.T)])
    z_mats = np.stack([hi_lo(wz), hi_lo(wz.T)])
    mx = np.arange(NX // 2 + 1)
    k2 = lambda m, n: (2 * np.pi * m / (0.5 * n)) ** 2
    squared = k2(mx, NX)[:, None, None] + k2(my, NY)[None, :, None] + k2(mz, NZ)[None, None, :]
    green = 4 * np.pi / (squared + 0.25)
    weight = np.where((mx == 0) | (mx == NX // 2), 1.0, 2.0) / NX
    green = green * weight[:, None, None]
    green = np.pad(green, ((0, 0), (0, YP - NY), (0, ZP - NZ)))
    green = np.concatenate([green, green], -1).astype(np.float32)
    return y_mats, z_mats, green


def split(x):
    hi = x.astype(jnp.bfloat16)
    return hi, (x - hi.astype(jnp.float32)).astype(jnp.bfloat16)


def dot(a, b):
    return lax.dot_general(a, b, (((1,), (0,)), ((), ())), preferred_element_type=jnp.float32)


def times_right(x, mat):
    hi, lo = split(x)
    return dot(hi, mat[0]) + dot(lo, mat[0]) + dot(hi, mat[1])


def times_left(mat, x):
    hi, lo = split(x)
    return dot(mat[0], hi) + dot(mat[0], lo) + dot(mat[1], hi)


C3, S3 = 0.5, math.sqrt(3) / 2
S5A, S5B, R5 = math.sin(2 * math.pi / 5), math.sin(4 * math.pi / 5), math.sqrt(5) / 4


def five_even(zero, one, two):
    total, apart = one + two, (one - two) * R5
    base = zero - total * 0.25
    return zero + total, base + apart, base - apart


def five_odd(one, two):
    return one * S5A + two * S5B, one * S5B - two * S5A


def five_waves(p):
    return five_even(p[0], p[1] + p[4], p[2] + p[3]) + five_odd(p[1] - p[4], p[2] - p[3])


def five_points(c):
    zero, one, two = five_even(*c[:3])
    up, down = five_odd(*c[3:])
    return [zero, one + up, two + down, two - down, one - up]


def wave_of(two, three, five):
    wave = next(m for m in range(NX) if (m % 2, m % 3, m % 5) == (two, three, five % 5))
    return min(wave, NX - wave)


def x_solve(p, green):
    grid = [[[p[(15 * a + 10 * b + 6 * c) % NX] for c in range(5)] for b in range(3)] for a in range(2)]
    back = []
    for two in range(2):
        rows = [[grid[0][b][c] - grid[1][b][c] if two else grid[0][b][c] + grid[1][b][c] for c in range(5)] for b in range(3)]
        both = [rows[1][c] + rows[2][c] for c in range(5)]
        flat = five_waves([rows[0][c] + both[c] for c in range(5)])
        cosine = five_waves([rows[0][c] - both[c] * C3 for c in range(5)])
        sine = five_waves([(rows[1][c] - rows[2][c]) * S3 for c in range(5)])
        k = lambda three, five: green[wave_of(two, three, five)]
        flat = [flat[0] * k(0, 0), flat[1] * k(0, 1), flat[2] * k(0, 2), flat[3] * k(0, 1), flat[4] * k(0, 2)]
        new_c, new_s = [cosine[0] * k(1, 0)] + [None] * 4, [sine[0] * k(1, 0)] + [None] * 4
        for five in (1, 2):
            cc, cs, sc, ss = cosine[five], cosine[five + 2], sine[five], sine[five + 2]
            x_up, x_down = (cc - ss) * k(1, five), (cc + ss) * k(1, -five)
            y_up, y_down = (sc + cs) * k(1, five), (sc - cs) * k(1, -five)
            new_c[five], new_s[five + 2] = x_up + x_down, x_down - x_up
            new_s[five], new_c[five + 2] = y_up + y_down, y_up - y_down
        flat, cosine, sine = five_points(flat), five_points(new_c), five_points(new_s)
        lines = [[flat[c] + cosine[c] for c in range(5)], [], []]
        for c in range(5):
            middle, side = flat[c] - cosine[c] * C3, sine[c] * S3
            lines[1].append(middle + side)
            lines[2].append(middle - side)
        back.append(lines)
    out = [None] * NX
    for a in range(2):
        for b in range(3):
            for c in range(5):
                plus, minus = back[0][b][c], back[1][b][c]
                out[(15 * a + 10 * b + 6 * c) % NX] = minus_or(plus, minus, a)
    return out


def minus_or(plus, minus, a):
    return plus - minus if a else plus + minus


def forward_yz(t, p_buf, g_buf, d_buf, y_ref, z_ref):
    planes = pl.ds(5 * t, 5)
    p = p_buf[planes].reshape(5 * YP, 128)
    turned = pltpu.roll(p, ZP, 1)
    low = lax.broadcasted_iota(jnp.int32, p.shape, 1) < ZP
    for half in range(2):
        both = jnp.where(low, p, turned) if half == 0 else jnp.where(low, turned, p)
        g = g_buf[half, planes].reshape(5 * YP, 256)
        s = times_right(jnp.concatenate([both, both], 1) * g, z_ref[0])
        d_buf[half, planes] = times_left(y_ref[0], s).reshape(5, YP, 256)


def middle_x(yt, d_buf, green_ref):
    rows = pl.ds(pl.multiple_of(8 * yt, 8), 8)
    green = [green_ref[m, rows, :] for m in range(16)]
    for lane in (0, 128):
        lanes = pl.ds(lane, 128)
        out = x_solve([d_buf[x // XH, x % XH, rows, lanes] for x in range(NX)], green)
        for x in range(NX):
            d_buf[x // XH, x % XH, rows, lanes] = out[x]


def inverse_yz(t, g_buf, d_buf, w, y_ref, z_ref):
    planes = pl.ds(5 * t, 5)
    sums = []
    for half in range(2):
        s = times_left(y_ref[1], d_buf[half, planes].reshape(5 * YP, 256))
        v = times_right(s, z_ref[1]) * (g_buf[half, planes].reshape(5 * YP, 256) * w)
        pair = v[:, :128] + v[:, 128:]
        sums.append(pair + pltpu.roll(pair, ZP, 1))
    low = lax.broadcasted_iota(jnp.int32, sums[0].shape, 1) < ZP
    return jnp.where(low, sums[0], sums[1]).reshape(5, YP, 128)


MESH = pl.DeviceIdType.MESH
SPOTS = 16
CHIPS = 32
RING = 8
ROWS = 24
WINDOW = 1920
TILES = 15


def device(orb, grid):
    return {"orb": orb, "grid": grid}


def remote(src, dst, sends, arrivals, target):
    return pltpu.make_async_remote_copy(
        src_ref=src, dst_ref=dst, send_sem=sends, recv_sem=arrivals, device_id=target, device_id_type=MESH
    )


def drain(ref, sem):
    pltpu.make_async_copy(ref, ref, sem).wait()


def cut_rows(flat, last, rows, points):
    lane = lax.broadcasted_iota(jnp.int32, (8, 128), 1)

    def cut(base, count, tile):
        for r in range(count):
            j, off = divmod(NZ * r, 128)
            both = tile(j) if off <= 128 - NZ else jnp.where(lane < off, tile(j + 1), tile(j))
            rows[pl.ds(base + 8 * r, 8), :] = pltpu.roll(both, 128 - off, 1) if off else both

    whole = points // WINDOW
    tail = points - points // 128 * 128
    last[...] = jnp.zeros((8, 128), jnp.float32)
    last[:, 0:tail] = flat[:, points - tail:points]

    @pl.loop(0, whole, unroll=6)
    def _(k):
        cut(
            pl.multiple_of(k * 256, 256), 32,
            lambda j: flat[:, pl.ds(pl.multiple_of(k * WINDOW + j * 128, 128), 128)],
        )

    end = whole * TILES
    cut(
        whole * 256, (points - whole * WINDOW) // NZ,
        lambda j: last[...] if end + j == points // 128 else flat[:, (end + j) * 128:(end + j + 1) * 128],
    )
    rows[8 * (NX * NY):8 * (NX * NY + YP - NY), :] = jnp.zeros((8 * (YP - NY), 128), jnp.float32)


def plane(rows, x, line):
    return rows[pl.ds(x * (8 * NY) + line, YP, stride=8), :]


def kernel(
    ground_ref, response_ref, density_ref, signs_ref, offsets_ref, y_hbm, z_hbm, green_hbm,
    out_ref,
    y_ref, z_ref, green_ref, flat, last, rows, g_buf, p_buf, q_buf, own_buf, d_own, d_far, e_out, e_in,
    term, pair_in, half_sum, plane_in, part_sum, ring_in, part_all, rho,
    in_sems, p_sems, e_send, e_recv, pair_sems, plane_send, plane_recv, ring_send, ring_recv, all_send, all_recv,
):
    orb, grid = lax.axis_index("orb"), lax.axis_index("grid")
    core = lax.rem(orb, 2)
    z_lo = lax.rem(orb // 2, 2)
    spot = orb // 4
    level = grid * 2 + z_lo
    left = device(lax.rem(orb + 63, 64), grid)
    right = device(lax.rem(orb + 1, 64), grid)
    partner = device(orb + 1 - 2 * core, grid)

    loads = (
        pltpu.make_async_copy(ground_ref, flat.at[0:NB], in_sems.at[0]),
        pltpu.make_async_copy(response_ref, flat.at[NB:NB + 1], in_sems.at[1]),
        pltpu.make_async_copy(density_ref, flat.at[NB + 1:NB + 2], in_sems.at[2]),
    )
    fixed = (
        pltpu.make_async_copy(y_hbm, y_ref, in_sems.at[3]),
        pltpu.make_async_copy(z_hbm, z_ref, in_sems.at[4]),
        pltpu.make_async_copy(green_hbm, green_ref, in_sems.at[5]),
    )
    for load in loads + fixed:
        load.start()

    def in_plane(d):
        other = lax.rem(spot + d, SPOTS)
        return other, device(other * 4 + lax.rem(orb, 4), grid)

    def in_chips(d):
        other = lax.rem(spot * 2 + core + d, CHIPS)
        return device(other // 2 * 4 + z_lo * 2 + lax.rem(other, 2), grid)

    def in_ring(d):
        other = lax.rem(level + d, RING)
        return device(spot * 4 + lax.rem(other, 2) * 2 + core, other // 2)

    barrier = pltpu.get_barrier_semaphore()

    def greet(target):
        pl.semaphore_signal(barrier, inc=1, device_id=target, device_id_type=MESH)

    for target in (left, right):
        greet(target)

    @pl.loop(1, CHIPS)
    def _(d):
        greet(in_chips(d))

    @pl.loop(1, RING)
    def _(d):
        greet(in_ring(d))

    for load in loads:
        load.wait()
    cut_rows(flat, last, rows, flat.shape[1])

    low = lax.broadcasted_iota(jnp.int32, (YP, 128), 1) < ZP
    own_sign = signs_ref[grid].astype(jnp.float32)

    def packed(i, line):
        return jnp.where(low, plane(rows, i, line), pltpu.roll(plane(rows, i + XH, line), ZP, 1))

    @pl.loop(0, XH)
    def _(i):
        p, own = packed(i, NB), packed(i, grid)
        p_buf[i] = p
        own_buf[i] = own
        term[pl.ds(2 * i, 2)] = (own * own_sign * p).reshape(2, ROWS, 128)

    term[2 * XH:CHIPS] = jnp.zeros((CHIPS - 2 * XH, ROWS, 128), jnp.float32)
    p_buf[0, NY:YP, :] = jnp.broadcast_to(offsets_ref[0, 1].astype(jnp.float32), (YP - NY, 128))
    pl.semaphore_wait(barrier, 2 + CHIPS - 1 + RING - 1)

    give_half = remote(term.at[pl.ds((1 - core) * SPOTS, SPOTS)], pair_in, pair_sems.at[0], pair_sems.at[1], partner)
    give_half.start()

    @pl.loop(0, XH)
    def _(i):
        for half in range(2):
            x = i + XH * half
            for pair in (0, 2):
                g = jnp.where(low, plane(rows, x, pair), pltpu.roll(plane(rows, x, pair + 1), ZP, 1))
                g_buf[half, i, :, 64 * pair:64 * pair + 128] = g

    give_half.wait()
    half_sum[...] = term[pl.ds(core * SPOTS, SPOTS)] + pair_in[...]

    @pl.loop(1, SPOTS)
    def _(d):
        other, target = in_plane(d)
        remote(half_sum.at[other], plane_in.at[d - 1], plane_send, plane_recv, target).start()

    give_p = remote(p_buf, q_buf, p_sems.at[0], p_sems.at[1], left)
    give_p.start()

    for load in fixed:
        load.wait()
    for t in range(3):
        forward_yz(t, p_buf, g_buf, d_own, y_ref, z_ref)

    drain(half_sum.at[pl.ds(0, SPOTS - 1)], plane_send)
    drain(plane_in, plane_recv)
    part = half_sum[spot]
    for d in range(SPOTS - 1):
        part = part + plane_in[d]
    part_sum[...] = part

    @pl.loop(1, RING)
    def _(d):
        remote(part_sum, ring_in.at[d - 1], ring_send, ring_recv, in_ring(d)).start()

    give_p.wait_recv()

    for t in range(3):
        forward_yz(t, q_buf, g_buf, d_far, y_ref, z_ref)

    drain(ring_in, ring_send)
    drain(ring_in, ring_recv)
    part = part_sum[...]
    for d in range(RING - 1):
        part = part + ring_in[d]
    part_all[...] = part
    mine = core * SPOTS + spot
    rho[mine] = part

    @pl.loop(1, CHIPS)
    def _(d):
        remote(part_all, rho.at[mine], all_send, all_recv, in_chips(d)).start()

    @pl.loop(0, YP // 8)
    def _(yt):
        middle_x(yt, d_far, green_ref)

    lane_q = lax.broadcasted_iota(jnp.int32, (1, 256), 1) // ZP
    signs = jnp.zeros((1, 256), jnp.float32)
    for q in range(NB):
        signs = jnp.where(lane_q == q, signs_ref[q].astype(jnp.float32), signs)
    lane_q = lane_q.astype(jnp.float32)
    far_offset = q_buf[0, NY:NY + 1, :]
    far_w = signs * (lane_q >= jnp.concatenate([far_offset, far_offset], 1)).astype(jnp.float32)
    own_offset = jnp.broadcast_to(offsets_ref[0, 0].astype(jnp.float32), (1, 256))
    own_w = signs * (lane_q >= own_offset).astype(jnp.float32)

    def e_copy(t):
        planes = pl.ds(5 * t, 5)
        return remote(e_out.at[planes], e_in.at[planes], e_send.at[t], e_recv.at[t], right)

    for t in range(3):
        e_out[pl.ds(5 * t, 5)] = inverse_yz(t, g_buf, d_far, far_w, y_ref, z_ref)
        e_copy(t).start()

    @pl.loop(0, XH)
    def _(i):
        own_buf[i] = own_buf[i] * (jnp.exp(jnp.log(packed(i, NB + 1)) * (-2.0 / 3.0)) * -XC_COEF)

    @pl.loop(0, YP // 8)
    def _(yt):
        middle_x(yt, d_own, green_ref)

    for t in range(3):
        e_out_t = inverse_yz(t, g_buf, d_own, own_w, y_ref, z_ref)
        e_copy(t).wait()
        e_in[pl.ds(5 * t, 5)] = (e_out_t + e_in[pl.ds(5 * t, 5)]) * -HYBRID

    drain(rho.at[pl.ds(0, CHIPS - 1)], all_send)
    drain(rho.at[pl.ds(0, CHIPS - 1)], all_recv)

    @pl.loop(0, XH)
    def _(i):
        total = own_buf[i] * rho[pl.ds(2 * i, 2)].reshape(YP, 128) + e_in[i]
        out_ref[i] = total[:NY, :NZ]
        out_ref[XH + i] = total[:NY, ZP:ZP + NZ]

    give_p.wait_send()


def per_device(ground_orbitals, occupation_signs, response_orbitals, window_offsets, ground_density):
    points = response_orbitals.shape[1]
    y_mats, z_mats, green = tables()
    vmem = pl.BlockSpec(memory_space=pltpu.VMEM)
    smem = pl.BlockSpec(memory_space=pltpu.SMEM)
    hbm = pl.BlockSpec(memory_space=pltpu.HBM)
    f32 = jnp.float32
    dma = pltpu.SemaphoreType.DMA
    grid_planes = pltpu.VMEM((XH, YP, 128), f32)
    wide_planes = pltpu.VMEM((2, XH, YP, 256), f32)

    def chunks(*count):
        return pltpu.VMEM((*count, ROWS, 128), f32)

    action = pl.pallas_call(
        kernel,
        out_shape=jax.ShapeDtypeStruct((NX, NY, NZ), f32),
        in_specs=[hbm, hbm, hbm, smem, smem, hbm, hbm, hbm],
        out_specs=vmem,
        scratch_shapes=[
            pltpu.VMEM(y_mats.shape, jnp.bfloat16), pltpu.VMEM(z_mats.shape, jnp.bfloat16), pltpu.VMEM(green.shape, f32),
            pltpu.VMEM((8, points), f32),
            pltpu.VMEM((8, 128), f32),
            pltpu.VMEM((8 * (NX * NY + YP - NY), 128), f32),
            wide_planes, grid_planes, grid_planes, grid_planes, wide_planes, wide_planes, grid_planes, grid_planes,
            chunks(CHIPS), chunks(SPOTS), chunks(SPOTS), chunks(SPOTS - 1), chunks(), chunks(RING - 1), chunks(), chunks(CHIPS),
            dma((6,)), dma((2,)), dma((3,)), dma((3,)), dma((2,)), dma, dma, dma, dma, dma, dma,
        ],
        compiler_params=pltpu.CompilerParams(
            collective_id=0, has_side_effects=True, vmem_limit_bytes=57 << 20
        ),
    )(
        ground_orbitals, response_orbitals, ground_density.reshape(1, points),
        occupation_signs, window_offsets, y_mats, z_mats, green,
    )
    return action.reshape(1, points)


def solution(mesh):
    placed = (P("orb", None), P("orb"), P(("orb", "grid"), None), P(("orb", "grid"), None), P())
    return jax.shard_map(
        per_device, mesh=mesh, in_specs=placed, out_specs=P(("orb", "grid"), None), check_vma=False
    )
```

```python
import math
import numpy as np
import ml_dtypes
import jax
import jax.numpy as jnp
from jax import lax
from jax.experimental import pallas as pl
from jax.experimental.pallas import tpu as pltpu
from jax.sharding import PartitionSpec as P

NX, NY, NZ = 30, 45, 60
NB = 4
YP, ZP = 48, 64
XH = NX // 2
XC_COEF = 0.3282
HYBRID = 0.25


def real_basis(n):
    j = np.arange(n)
    rows, waves = [np.ones(n) / math.sqrt(n)], [0]
    for m in range(1, (n - 1) // 2 + 1):
        rows += [math.sqrt(2 / n) * np.cos(2 * np.pi * m * j / n), math.sqrt(2 / n) * np.sin(2 * np.pi * m * j / n)]
        waves += [m, m]
    if n % 2 == 0:
        rows.append(np.cos(np.pi * j) / math.sqrt(n))
        waves.append(n // 2)
    return np.array(rows), np.array(waves)


def padded(matrix, size):
    return np.pad(matrix, ((0, size - matrix.shape[0]), (0, size - matrix.shape[1])))


def hi_lo(matrix):
    hi = matrix.astype(ml_dtypes.bfloat16)
    lo = (matrix - hi.astype(np.float64)).astype(ml_dtypes.bfloat16)
    return np.stack([hi, lo])


def tables():
    ty, my = real_basis(NY)
    tz, mz = real_basis(NZ)
    ty, tz = padded(ty, YP), padded(tz, ZP)
    wy = np.kron(np.eye(5), ty)
    wz = np.kron(np.eye(NB), tz.T)
    y_mats = np.stack([hi_lo(wy), hi_lo(wy.T)])
    z_mats = np.stack([hi_lo(wz), hi_lo(wz.T)])
    mx = np.arange(NX // 2 + 1)
    k2 = lambda m, n: (2 * np.pi * m / (0.5 * n)) ** 2
    squared = k2(mx, NX)[:, None, None] + k2(my, NY)[None, :, None] + k2(mz, NZ)[None, None, :]
    green = 4 * np.pi / (squared + 0.25)
    weight = np.where((mx == 0) | (mx == NX // 2), 1.0, 2.0) / NX
    green = green * weight[:, None, None]
    green = np.pad(green, ((0, 0), (0, YP - NY), (0, ZP - NZ)))
    green = np.concatenate([green, green], -1).astype(np.float32)
    return y_mats, z_mats, green


def split(x):
    hi = x.astype(jnp.bfloat16)
    return hi, (x - hi.astype(jnp.float32)).astype(jnp.bfloat16)


def dot(a, b):
    return lax.dot_general(a, b, (((1,), (0,)), ((), ())), preferred_element_type=jnp.float32)


def times_right(x, mat):
    hi, lo = split(x)
    return dot(hi, mat[0]) + dot(lo, mat[0]) + dot(hi, mat[1])


def times_left(mat, x):
    hi, lo = split(x)
    return dot(mat[0], hi) + dot(mat[0], lo) + dot(mat[1], hi)


C3, S3 = 0.5, math.sqrt(3) / 2
S5A, S5B, R5 = math.sin(2 * math.pi / 5), math.sin(4 * math.pi / 5), math.sqrt(5) / 4


def five_even(zero, one, two):
    total, apart = one + two, (one - two) * R5
    base = zero - total * 0.25
    return zero + total, base + apart, base - apart


def five_odd(one, two):
    return one * S5A + two * S5B, one * S5B - two * S5A


def five_waves(p):
    return five_even(p[0], p[1] + p[4], p[2] + p[3]) + five_odd(p[1] - p[4], p[2] - p[3])


def five_points(c):
    zero, one, two = five_even(*c[:3])
    up, down = five_odd(*c[3:])
    return [zero, one + up, two + down, two - down, one - up]


def wave_of(two, three, five):
    wave = next(m for m in range(NX) if (m % 2, m % 3, m % 5) == (two, three, five % 5))
    return min(wave, NX - wave)


def x_solve(p, green):
    grid = [[[p[(15 * a + 10 * b + 6 * c) % NX] for c in range(5)] for b in range(3)] for a in range(2)]
    back = []
    for two in range(2):
        rows = [[grid[0][b][c] - grid[1][b][c] if two else grid[0][b][c] + grid[1][b][c] for c in range(5)] for b in range(3)]
        both = [rows[1][c] + rows[2][c] for c in range(5)]
        flat = five_waves([rows[0][c] + both[c] for c in range(5)])
        cosine = five_waves([rows[0][c] - both[c] * C3 for c in range(5)])
        sine = five_waves([(rows[1][c] - rows[2][c]) * S3 for c in range(5)])
        k = lambda three, five: green[wave_of(two, three, five)]
        flat = [flat[0] * k(0, 0), flat[1] * k(0, 1), flat[2] * k(0, 2), flat[3] * k(0, 1), flat[4] * k(0, 2)]
        new_c, new_s = [cosine[0] * k(1, 0)] + [None] * 4, [sine[0] * k(1, 0)] + [None] * 4
        for five in (1, 2):
            cc, cs, sc, ss = cosine[five], cosine[five + 2], sine[five], sine[five + 2]
            x_up, x_down = (cc - ss) * k(1, five), (cc + ss) * k(1, -five)
            y_up, y_down = (sc + cs) * k(1, five), (sc - cs) * k(1, -five)
            new_c[five], new_s[five + 2] = x_up + x_down, x_down - x_up
            new_s[five], new_c[five + 2] = y_up + y_down, y_up - y_down
        flat, cosine, sine = five_points(flat), five_points(new_c), five_points(new_s)
        lines = [[flat[c] + cosine[c] for c in range(5)], [], []]
        for c in range(5):
            middle, side = flat[c] - cosine[c] * C3, sine[c] * S3
            lines[1].append(middle + side)
            lines[2].append(middle - side)
        back.append(lines)
    out = [None] * NX
    for a in range(2):
        for b in range(3):
            for c in range(5):
                plus, minus = back[0][b][c], back[1][b][c]
                out[(15 * a + 10 * b + 6 * c) % NX] = minus_or(plus, minus, a)
    return out


def minus_or(plus, minus, a):
    return plus - minus if a else plus + minus


def forward_yz(t, p_buf, g_buf, d_buf, y_ref, z_ref):
    planes = pl.ds(5 * t, 5)
    p = p_buf[planes].reshape(5 * YP, 128)
    turned = pltpu.roll(p, ZP, 1)
    low = lax.broadcasted_iota(jnp.int32, p.shape, 1) < ZP
    for half in range(2):
        both = jnp.where(low, p, turned) if half == 0 else jnp.where(low, turned, p)
        g = g_buf[half, planes].reshape(5 * YP, 256)
        s = times_right(jnp.concatenate([both, both], 1) * g, z_ref[0])
        d_buf[half, planes] = times_left(y_ref[0], s).reshape(5, YP, 256)


def middle_x(yt, d_buf, green_ref):
    rows = pl.ds(pl.multiple_of(8 * yt, 8), 8)
    green = [green_ref[m, rows, :] for m in range(16)]
    for lane in (0, 128):
        lanes = pl.ds(lane, 128)
        out = x_solve([d_buf[x // XH, x % XH, rows, lanes] for x in range(NX)], green)
        for x in range(NX):
            d_buf[x // XH, x % XH, rows, lanes] = out[x]


def inverse_yz(t, g_buf, d_buf, w, y_ref, z_ref):
    planes = pl.ds(5 * t, 5)
    sums = []
    for half in range(2):
        s = times_left(y_ref[1], d_buf[half, planes].reshape(5 * YP, 256))
        v = times_right(s, z_ref[1]) * (g_buf[half, planes].reshape(5 * YP, 256) * w)
        pair = v[:, :128] + v[:, 128:]
        sums.append(pair + pltpu.roll(pair, ZP, 1))
    low = lax.broadcasted_iota(jnp.int32, sums[0].shape, 1) < ZP
    return jnp.where(low, sums[0], sums[1]).reshape(5, YP, 128)


MESH = pl.DeviceIdType.MESH
SPOTS = 16
CHIPS = 32
RING = 8
ROWS = 24
WINDOW = 1920
TILES = 15
PIECES = 3
UNROLL = 7


def device(orb, grid):
    return {"orb": orb, "grid": grid}


def remote(src, dst, sends, arrivals, target):
    return pltpu.make_async_remote_copy(
        src_ref=src, dst_ref=dst, send_sem=sends, recv_sem=arrivals, device_id=target, device_id_type=MESH
    )


def drain(ref, sem):
    pltpu.make_async_copy(ref, ref, sem).wait()


def cut_rows(flat, last, rows, points, arrive, greetings):
    lane = lax.broadcasted_iota(jnp.int32, (8, 128), 1)

    def cut(base, count, tile):
        for r in range(count):
            j, off = divmod(NZ * r, 128)
            both = tile(j) if off <= 128 - NZ else jnp.where(lane < off, tile(j + 1), tile(j))
            rows[pl.ds(base + 8 * r, 8), :] = pltpu.roll(both, 128 - off, 1) if off else both

    whole = points // WINDOW
    tail = points - points // 128 * 128
    for piece in range(PIECES):
        arrive(piece)

        @pl.loop(0, whole // PIECES // UNROLL)
        def _(step):
            for u in range(UNROLL):
                k = piece * (whole // PIECES) + step * UNROLL + u
                greetings[piece](step * UNROLL + u)
                cut(
                    pl.multiple_of(k * 256, 256), 32,
                    lambda j: flat[:, pl.ds(pl.multiple_of(k * WINDOW + j * 128, 128), 128)],
                )

    end = whole * TILES
    last[...] = jnp.zeros((8, 128), jnp.float32)
    last[:, 0:tail] = flat[:, points - tail:points]
    cut(
        whole * 256, (points - whole * WINDOW) // NZ,
        lambda j: last[...] if end + j == points // 128 else flat[:, (end + j) * 128:(end + j + 1) * 128],
    )
    rows[8 * (NX * NY):8 * (NX * NY + YP - NY), :] = jnp.zeros((8 * (YP - NY), 128), jnp.float32)


def plane(rows, x, line):
    return rows[pl.ds(x * (8 * NY) + line, YP, stride=8), :]


def kernel(
    ground_ref, response_ref, density_ref, signs_ref, offsets_ref, y_hbm, z_hbm, green_hbm,
    out_ref,
    y_ref, z_ref, green_ref, flat, last, rows, g_buf, p_buf, q_buf, own_buf, d_own, d_far, e_out, e_in,
    term, pair_in, half_sum, plane_in, part_sum, ring_in, part_all, rho,
    in_sems, p_sems, e_send, e_recv, pair_sems, plane_send, plane_recv, ring_send, ring_recv, all_send, all_recv,
):
    orb, grid = lax.axis_index("orb"), lax.axis_index("grid")
    core = lax.rem(orb, 2)
    z_lo = lax.rem(orb // 2, 2)
    spot = orb // 4
    level = grid * 2 + z_lo
    left = device(lax.rem(orb + 63, 64), grid)
    right = device(lax.rem(orb + 1, 64), grid)
    partner = device(orb + 1 - 2 * core, grid)

    points = flat.shape[1]
    cuts = [piece * (points // WINDOW // PIECES) * WINDOW for piece in range(PIECES)] + [points]
    lines = ((ground_ref, 0, NB), (response_ref, NB, 1), (density_ref, NB + 1, 1))
    loads = [
        [
            pltpu.make_async_copy(
                source.at[:, cuts[piece]:cuts[piece + 1]],
                flat.at[first:first + count, cuts[piece]:cuts[piece + 1]],
                in_sems.at[piece, at],
            )
            for at, (source, first, count) in enumerate(lines)
        ]
        for piece in range(PIECES)
    ]
    fixed = (
        pltpu.make_async_copy(y_hbm, y_ref, in_sems.at[PIECES, 0]),
        pltpu.make_async_copy(z_hbm, z_ref, in_sems.at[PIECES, 1]),
        pltpu.make_async_copy(green_hbm, green_ref, in_sems.at[PIECES, 2]),
    )
    for load in sum(loads, []) + list(fixed):
        load.start()

    def in_plane(d):
        other = lax.rem(spot + d, SPOTS)
        return other, device(other * 4 + lax.rem(orb, 4), grid)

    def in_chips(d):
        other = lax.rem(spot * 2 + core + d, CHIPS)
        return device(other // 2 * 4 + z_lo * 2 + lax.rem(other, 2), grid)

    def in_ring(d):
        other = lax.rem(level + d, RING)
        return device(spot * 4 + lax.rem(other, 2) * 2 + core, other // 2)

    barrier = pltpu.get_barrier_semaphore()

    def greet(target):
        pl.semaphore_signal(barrier, inc=1, device_id=target, device_id_type=MESH)

    for target in (left, right):
        greet(target)

    @pl.loop(1, CHIPS - 28)
    def _(d):
        greet(in_chips(d))

    @pl.loop(1, RING)
    def _(d):
        greet(in_ring(d))

    def arrive(piece):
        for load in loads[piece]:
            load.wait()

    greetings = (
        lambda at: greet(in_chips(CHIPS - 28 + at)),
        lambda at: greet(in_chips(CHIPS - 14 + at)),
        lambda at: None,
    )
    cut_rows(flat, last, rows, points, arrive, greetings)

    low = lax.broadcasted_iota(jnp.int32, (YP, 128), 1) < ZP
    own_sign = signs_ref[grid].astype(jnp.float32)

    def packed(i, line):
        return jnp.where(low, plane(rows, i, line), pltpu.roll(plane(rows, i + XH, line), ZP, 1))

    @pl.loop(0, XH)
    def _(i):
        p, own = packed(i, NB), packed(i, grid)
        p_buf[i] = p
        own_buf[i] = own
        term[pl.ds(2 * i, 2)] = (own * own_sign * p).reshape(2, ROWS, 128)

    term[2 * XH:CHIPS] = jnp.zeros((CHIPS - 2 * XH, ROWS, 128), jnp.float32)
    p_buf[0, NY:YP, :] = jnp.broadcast_to(offsets_ref[0, 1].astype(jnp.float32), (YP - NY, 128))
    pl.semaphore_wait(barrier, 2 + CHIPS - 1 + RING - 1)

    give_half = remote(term.at[pl.ds((1 - core) * SPOTS, SPOTS)], pair_in, pair_sems.at[0], pair_sems.at[1], partner)
    give_half.start()

    give_p = remote(p_buf, q_buf, p_sems.at[0], p_sems.at[1], left)
    give_p.start()

    @pl.loop(0, XH)
    def _(i):
        for half in range(2):
            x = i + XH * half
            for pair in (0, 2):
                g = jnp.where(low, plane(rows, x, pair), pltpu.roll(plane(rows, x, pair + 1), ZP, 1))
                g_buf[half, i, :, 64 * pair:64 * pair + 128] = g

    give_half.wait()
    half_sum[...] = term[pl.ds(core * SPOTS, SPOTS)] + pair_in[...]

    @pl.loop(1, SPOTS)
    def _(d):
        other, target = in_plane(d)
        remote(half_sum.at[other], plane_in.at[d - 1], plane_send, plane_recv, target).start()

    for load in fixed:
        load.wait()
    for t in range(3):
        forward_yz(t, p_buf, g_buf, d_own, y_ref, z_ref)

    @pl.loop(0, YP // 8)
    def _(yt):
        middle_x(yt, d_own, green_ref)

    @pl.loop(0, XH)
    def _(i):
        own_buf[i] = own_buf[i] * (jnp.exp(jnp.log(packed(i, NB + 1)) * (-2.0 / 3.0)) * -XC_COEF)

    give_p.wait_recv()

    for t in range(3):
        forward_yz(t, q_buf, g_buf, d_far, y_ref, z_ref)

    drain(half_sum.at[pl.ds(0, SPOTS - 1)], plane_send)
    drain(plane_in, plane_recv)
    part = half_sum[spot]
    for d in range(SPOTS - 1):
        part = part + plane_in[d]
    part_sum[...] = part

    @pl.loop(1, RING)
    def _(d):
        remote(part_sum, ring_in.at[d - 1], ring_send, ring_recv, in_ring(d)).start()

    @pl.loop(0, YP // 8)
    def _(yt):
        middle_x(yt, d_far, green_ref)

    lane_q = lax.broadcasted_iota(jnp.int32, (1, 256), 1) // ZP
    signs = jnp.zeros((1, 256), jnp.float32)
    for q in range(NB):
        signs = jnp.where(lane_q == q, signs_ref[q].astype(jnp.float32), signs)
    lane_q = lane_q.astype(jnp.float32)
    far_offset = q_buf[0, NY:NY + 1, :]
    far_w = signs * (lane_q >= jnp.concatenate([far_offset, far_offset], 1)).astype(jnp.float32)
    own_offset = jnp.broadcast_to(offsets_ref[0, 0].astype(jnp.float32), (1, 256))
    own_w = signs * (lane_q >= own_offset).astype(jnp.float32)

    def e_copy(t):
        planes = pl.ds(5 * t, 5)
        return remote(e_out.at[planes], e_in.at[planes], e_send.at[t], e_recv.at[t], right)

    for t in range(3):
        e_out[pl.ds(5 * t, 5)] = inverse_yz(t, g_buf, d_far, far_w, y_ref, z_ref)
        e_copy(t).start()

    drain(ring_in, ring_send)
    drain(ring_in, ring_recv)
    part = part_sum[...]
    for d in range(RING - 1):
        part = part + ring_in[d]
    part_all[...] = part
    mine = core * SPOTS + spot
    rho[mine] = part

    @pl.loop(1, CHIPS)
    def _(d):
        remote(part_all, rho.at[mine], all_send, all_recv, in_chips(d)).start()

    for t in range(3):
        e_out_t = inverse_yz(t, g_buf, d_own, own_w, y_ref, z_ref)
        e_copy(t).wait()
        e_in[pl.ds(5 * t, 5)] = (e_out_t + e_in[pl.ds(5 * t, 5)]) * -HYBRID

    drain(rho.at[pl.ds(0, CHIPS - 1)], all_send)
    drain(rho.at[pl.ds(0, CHIPS - 1)], all_recv)

    @pl.loop(0, XH)
    def _(i):
        total = own_buf[i] * rho[pl.ds(2 * i, 2)].reshape(YP, 128) + e_in[i]
        out_ref[i] = total[:NY, :NZ]
        out_ref[XH + i] = total[:NY, ZP:ZP + NZ]

    give_p.wait_send()


def per_device(ground_orbitals, occupation_signs, response_orbitals, window_offsets, ground_density):
    points = response_orbitals.shape[1]
    y_mats, z_mats, green = tables()
    vmem = pl.BlockSpec(memory_space=pltpu.VMEM)
    smem = pl.BlockSpec(memory_space=pltpu.SMEM)
    hbm = pl.BlockSpec(memory_space=pltpu.HBM)
    f32 = jnp.float32
    dma = pltpu.SemaphoreType.DMA
    grid_planes = pltpu.VMEM((XH, YP, 128), f32)
    wide_planes = pltpu.VMEM((2, XH, YP, 256), f32)

    def chunks(*count):
        return pltpu.VMEM((*count, ROWS, 128), f32)

    action = pl.pallas_call(
        kernel,
        out_shape=jax.ShapeDtypeStruct((NX, NY, NZ), f32),
        in_specs=[hbm, hbm, hbm, smem, smem, hbm, hbm, hbm],
        out_specs=vmem,
        scratch_shapes=[
            pltpu.VMEM(y_mats.shape, jnp.bfloat16), pltpu.VMEM(z_mats.shape, jnp.bfloat16), pltpu.VMEM(green.shape, f32),
            pltpu.VMEM((8, points), f32),
            pltpu.VMEM((8, 128), f32),
            pltpu.VMEM((8 * (NX * NY + YP - NY), 128), f32),
            wide_planes, grid_planes, grid_planes, grid_planes, wide_planes, wide_planes, grid_planes, grid_planes,
            chunks(CHIPS), chunks(SPOTS), chunks(SPOTS), chunks(SPOTS - 1), chunks(), chunks(RING - 1), chunks(), chunks(CHIPS),
            dma((PIECES + 1, 3)), dma((2,)), dma((3,)), dma((3,)), dma((2,)), dma, dma, dma, dma, dma, dma,
        ],
        compiler_params=pltpu.CompilerParams(
            collective_id=0, has_side_effects=True, vmem_limit_bytes=57 << 20
        ),
    )(
        ground_orbitals, response_orbitals, ground_density.reshape(1, points),
        occupation_signs, window_offsets, y_mats, z_mats, green,
    )
    return action.reshape(1, points)


def solution(mesh):
    placed = (P("orb", None), P("orb"), P(("orb", "grid"), None), P(("orb", "grid"), None), P())
    return jax.shard_map(
        per_device, mesh=mesh, in_specs=placed, out_specs=P(("orb", "grid"), None), check_vma=False
    )
```

```python
import math
import numpy as np
import ml_dtypes
import jax
import jax.numpy as jnp
from jax import lax
from jax.experimental import pallas as pl
from jax.experimental.pallas import tpu as pltpu
from jax.sharding import PartitionSpec as P

NX, NY, NZ = 30, 45, 60
NB = 4
YP, ZP = 48, 64
XH = NX // 2
XC_COEF = 0.3282
HYBRID = 0.25


def real_basis(n):
    j = np.arange(n)
    rows, waves = [np.ones(n) / math.sqrt(n)], [0]
    for m in range(1, (n - 1) // 2 + 1):
        rows += [math.sqrt(2 / n) * np.cos(2 * np.pi * m * j / n), math.sqrt(2 / n) * np.sin(2 * np.pi * m * j / n)]
        waves += [m, m]
    if n % 2 == 0:
        rows.append(np.cos(np.pi * j) / math.sqrt(n))
        waves.append(n // 2)
    return np.array(rows), np.array(waves)


def padded(matrix, size):
    return np.pad(matrix, ((0, size - matrix.shape[0]), (0, size - matrix.shape[1])))


def hi_lo(matrix):
    hi = matrix.astype(ml_dtypes.bfloat16)
    lo = (matrix - hi.astype(np.float64)).astype(ml_dtypes.bfloat16)
    return np.stack([hi, lo])


def tables():
    ty, my = real_basis(NY)
    tz, mz = real_basis(NZ)
    ty, tz = padded(ty, YP), padded(tz, ZP)
    wy = np.kron(np.eye(5), ty)
    wz = np.kron(np.eye(NB), tz.T)
    y_mats = np.stack([hi_lo(wy), hi_lo(wy.T)])
    z_mats = np.stack([hi_lo(wz), hi_lo(wz.T)])
    mx = np.arange(NX // 2 + 1)
    k2 = lambda m, n: (2 * np.pi * m / (0.5 * n)) ** 2
    squared = k2(mx, NX)[:, None, None] + k2(my, NY)[None, :, None] + k2(mz, NZ)[None, None, :]
    green = 4 * np.pi / (squared + 0.25)
    weight = np.where((mx == 0) | (mx == NX // 2), 1.0, 2.0) / NX
    green = green * weight[:, None, None]
    green = np.pad(green, ((0, 0), (0, YP - NY), (0, ZP - NZ)))
    green = np.concatenate([green, green], -1).astype(np.float32)
    return y_mats, z_mats, green


def split(x):
    hi = x.astype(jnp.bfloat16)
    return hi, (x - hi.astype(jnp.float32)).astype(jnp.bfloat16)


def dot(a, b):
    return lax.dot_general(a, b, (((1,), (0,)), ((), ())), preferred_element_type=jnp.float32)


def times_right(x, mat):
    hi, lo = split(x)
    return dot(hi, mat[0]) + dot(lo, mat[0]) + dot(hi, mat[1])


def times_left(mat, x):
    hi, lo = split(x)
    return dot(mat[0], hi) + dot(mat[0], lo) + dot(mat[1], hi)


C3, S3 = 0.5, math.sqrt(3) / 2
S5A, S5B, R5 = math.sin(2 * math.pi / 5), math.sin(4 * math.pi / 5), math.sqrt(5) / 4


def five_even(zero, one, two):
    total, apart = one + two, (one - two) * R5
    base = zero - total * 0.25
    return zero + total, base + apart, base - apart


def five_odd(one, two):
    return one * S5A + two * S5B, one * S5B - two * S5A


def five_waves(p):
    return five_even(p[0], p[1] + p[4], p[2] + p[3]) + five_odd(p[1] - p[4], p[2] - p[3])


def five_points(c):
    zero, one, two = five_even(*c[:3])
    up, down = five_odd(*c[3:])
    return [zero, one + up, two + down, two - down, one - up]


def wave_of(two, three, five):
    wave = next(m for m in range(NX) if (m % 2, m % 3, m % 5) == (two, three, five % 5))
    return min(wave, NX - wave)


def x_solve(p, green):
    grid = [[[p[(15 * a + 10 * b + 6 * c) % NX] for c in range(5)] for b in range(3)] for a in range(2)]
    back = []
    for two in range(2):
        rows = [[grid[0][b][c] - grid[1][b][c] if two else grid[0][b][c] + grid[1][b][c] for c in range(5)] for b in range(3)]
        both = [rows[1][c] + rows[2][c] for c in range(5)]
        flat = five_waves([rows[0][c] + both[c] for c in range(5)])
        cosine = five_waves([rows[0][c] - both[c] * C3 for c in range(5)])
        sine = five_waves([(rows[1][c] - rows[2][c]) * S3 for c in range(5)])
        k = lambda three, five: green[wave_of(two, three, five)]
        flat = [flat[0] * k(0, 0), flat[1] * k(0, 1), flat[2] * k(0, 2), flat[3] * k(0, 1), flat[4] * k(0, 2)]
        new_c, new_s = [cosine[0] * k(1, 0)] + [None] * 4, [sine[0] * k(1, 0)] + [None] * 4
        for five in (1, 2):
            cc, cs, sc, ss = cosine[five], cosine[five + 2], sine[five], sine[five + 2]
            x_up, x_down = (cc - ss) * k(1, five), (cc + ss) * k(1, -five)
            y_up, y_down = (sc + cs) * k(1, five), (sc - cs) * k(1, -five)
            new_c[five], new_s[five + 2] = x_up + x_down, x_down - x_up
            new_s[five], new_c[five + 2] = y_up + y_down, y_up - y_down
        flat, cosine, sine = five_points(flat), five_points(new_c), five_points(new_s)
        lines = [[flat[c] + cosine[c] for c in range(5)], [], []]
        for c in range(5):
            middle, side = flat[c] - cosine[c] * C3, sine[c] * S3
            lines[1].append(middle + side)
            lines[2].append(middle - side)
        back.append(lines)
    out = [None] * NX
    for a in range(2):
        for b in range(3):
            for c in range(5):
                plus, minus = back[0][b][c], back[1][b][c]
                out[(15 * a + 10 * b + 6 * c) % NX] = minus_or(plus, minus, a)
    return out


def minus_or(plus, minus, a):
    return plus - minus if a else plus + minus


def forward_yz(t, p_buf, g_buf, d_buf, y_ref, z_ref):
    planes = pl.ds(5 * t, 5)
    p = p_buf[planes].reshape(5 * YP, 128)
    turned = pltpu.roll(p, ZP, 1)
    low = lax.broadcasted_iota(jnp.int32, p.shape, 1) < ZP
    for half in range(2):
        both = jnp.where(low, p, turned) if half == 0 else jnp.where(low, turned, p)
        g = g_buf[half, planes].reshape(5 * YP, 256)
        s = times_right(jnp.concatenate([both, both], 1) * g, z_ref[0])
        d_buf[half, planes] = times_left(y_ref[0], s).reshape(5, YP, 256)


def middle_x(yt, d_buf, green_ref):
    rows = pl.ds(pl.multiple_of(8 * yt, 8), 8)
    green = [green_ref[m, rows, :] for m in range(16)]
    for lane in (0, 128):
        lanes = pl.ds(lane, 128)
        out = x_solve([d_buf[x // XH, x % XH, rows, lanes] for x in range(NX)], green)
        for x in range(NX):
            d_buf[x // XH, x % XH, rows, lanes] = out[x]


def inverse_yz(t, g_buf, d_buf, w, y_ref, z_ref):
    planes = pl.ds(5 * t, 5)
    sums = []
    for half in range(2):
        s = times_left(y_ref[1], d_buf[half, planes].reshape(5 * YP, 256))
        v = times_right(s, z_ref[1]) * (g_buf[half, planes].reshape(5 * YP, 256) * w)
        pair = v[:, :128] + v[:, 128:]
        sums.append(pair + pltpu.roll(pair, ZP, 1))
    low = lax.broadcasted_iota(jnp.int32, sums[0].shape, 1) < ZP
    return jnp.where(low, sums[0], sums[1]).reshape(5, YP, 128)


MESH = pl.DeviceIdType.MESH
SPOTS = 16
CHIPS = 32
RING = 8
ROWS = 24
WINDOW = 1920
TILES = 15
PIECES = 3
UNROLL = 7


def device(orb, grid):
    return {"orb": orb, "grid": grid}


def remote(src, dst, sends, arrivals, target):
    return pltpu.make_async_remote_copy(
        src_ref=src, dst_ref=dst, send_sem=sends, recv_sem=arrivals, device_id=target, device_id_type=MESH
    )


def drain(ref, sem):
    pltpu.make_async_copy(ref, ref, sem).wait()


def cut_rows(flat, last, rows, points, arrive, greetings):
    lane = lax.broadcasted_iota(jnp.int32, (8, 128), 1)

    def cut(base, count, tile):
        for r in range(count):
            j, off = divmod(NZ * r, 128)
            both = tile(j) if off <= 128 - NZ else jnp.where(lane < off, tile(j + 1), tile(j))
            rows[pl.ds(base + 8 * r, 8), :] = pltpu.roll(both, 128 - off, 1) if off else both

    whole = points // WINDOW
    tail = points - points // 128 * 128
    for piece in range(PIECES):
        arrive(piece)

        @pl.loop(0, whole // PIECES // UNROLL)
        def _(step):
            for u in range(UNROLL):
                k = piece * (whole // PIECES) + step * UNROLL + u
                greetings[piece](step * UNROLL + u)
                cut(
                    pl.multiple_of(k * 256, 256), 32,
                    lambda j: flat[:, pl.ds(pl.multiple_of(k * WINDOW + j * 128, 128), 128)],
                )

    end = whole * TILES
    last[...] = jnp.zeros((8, 128), jnp.float32)
    last[:, 0:tail] = flat[:, points - tail:points]
    cut(
        whole * 256, (points - whole * WINDOW) // NZ,
        lambda j: last[...] if end + j == points // 128 else flat[:, (end + j) * 128:(end + j + 1) * 128],
    )
    rows[8 * (NX * NY):8 * (NX * NY + YP - NY), :] = jnp.zeros((8 * (YP - NY), 128), jnp.float32)


def join_rows(lines, flat):
    lane = lax.broadcasted_iota(jnp.int32, (8, 128), 1)

    @pl.loop(0, flat.shape[0] // (8 * TILES))
    def _(m):
        turned = []
        for r in range(32):
            line = lines[pl.ds(256 * m + r, 8, stride=32), :]
            off = NZ * r % 128
            turned.append(pltpu.roll(line, off, 1) if off else line)
        for t in range(TILES):
            pieces = [r for r in range(32) if NZ * r < 128 * (t + 1) and NZ * (r + 1) > 128 * t]
            tile = turned[pieces[0]]
            for r in pieces[1:]:
                tile = jnp.where(lane >= NZ * r - 128 * t, turned[r], tile)
            flat[pl.ds(8 * TILES * m + t, 8, stride=TILES), :] = tile


def plane(rows, x, line):
    return rows[pl.ds(x * (8 * NY) + line, YP, stride=8), :]


def kernel(
    ground_ref, response_ref, density_ref, signs_ref, offsets_ref, y_hbm, z_hbm, green_hbm,
    out_ref,
    y_ref, z_ref, green_ref, flat, last, rows, g_buf, p_buf, q_buf, own_buf, d_own, d_far, e_out, e_in, e_own,
    lines_out, term, pair_in, half_sum, plane_in, part_sum, ring_in, part_all, rho,
    in_sems, p_sems, e_send, e_recv, pair_sems, plane_send, plane_recv, ring_send, ring_recv, all_send, all_recv, swap_sems,
):
    orb, grid = lax.axis_index("orb"), lax.axis_index("grid")
    core = lax.rem(orb, 2)
    z_lo = lax.rem(orb // 2, 2)
    spot = orb // 4
    level = grid * 2 + z_lo
    left = device(lax.rem(orb + 63, 64), grid)
    right = device(lax.rem(orb + 1, 64), grid)
    partner = device(orb + 1 - 2 * core, grid)

    points = flat.shape[1]
    cuts = [piece * (points // WINDOW // PIECES) * WINDOW for piece in range(PIECES)] + [points]
    lines = ((ground_ref, 0, NB), (response_ref, NB, 1), (density_ref, NB + 1, 1))
    loads = [
        [
            pltpu.make_async_copy(
                source.at[:, cuts[piece]:cuts[piece + 1]] if at < 2 else source.at[cuts[piece]:cuts[piece + 1]],
                flat.at[first:first + count, cuts[piece]:cuts[piece + 1]] if at < 2 else flat.at[first, cuts[piece]:cuts[piece + 1]],
                in_sems.at[piece, at],
            )
            for at, (source, first, count) in enumerate(lines)
        ]
        for piece in range(PIECES)
    ]
    fixed = (
        pltpu.make_async_copy(y_hbm, y_ref, in_sems.at[PIECES, 0]),
        pltpu.make_async_copy(z_hbm, z_ref, in_sems.at[PIECES, 1]),
        pltpu.make_async_copy(green_hbm, green_ref, in_sems.at[PIECES, 2]),
    )
    for load in sum(loads, []) + list(fixed):
        load.start()

    def in_plane(d):
        other = lax.rem(spot + d, SPOTS)
        return other, device(other * 4 + lax.rem(orb, 4), grid)

    def in_chips(d):
        other = lax.rem(spot * 2 + core + d, CHIPS)
        return device(other // 2 * 4 + z_lo * 2 + lax.rem(other, 2), grid)

    def in_ring(d):
        other = lax.rem(level + d, RING)
        return device(spot * 4 + lax.rem(other, 2) * 2 + core, other // 2)

    barrier = pltpu.get_barrier_semaphore()

    def greet(target):
        pl.semaphore_signal(barrier, inc=1, device_id=target, device_id_type=MESH)

    for target in (left, right):
        greet(target)

    @pl.loop(1, CHIPS - 28)
    def _(d):
        greet(in_chips(d))

    @pl.loop(1, RING)
    def _(d):
        greet(in_ring(d))

    def arrive(piece):
        for load in loads[piece]:
            load.wait()

    greetings = (
        lambda at: greet(in_chips(CHIPS - 28 + at)),
        lambda at: greet(in_chips(CHIPS - 14 + at)),
        lambda at: None,
    )
    cut_rows(flat, last, rows, points, arrive, greetings)

    low = lax.broadcasted_iota(jnp.int32, (YP, 128), 1) < ZP
    own_sign = signs_ref[grid].astype(jnp.float32)

    def packed(i, line):
        return jnp.where(low, plane(rows, i, line), pltpu.roll(plane(rows, i + XH, line), ZP, 1))

    @pl.loop(0, XH)
    def _(i):
        p, own = packed(i, NB), packed(i, grid)
        p_buf[i] = p
        own_buf[i] = own
        term[pl.ds(2 * i, 2)] = (own * own_sign * p).reshape(2, ROWS, 128)

    term[2 * XH:CHIPS] = jnp.zeros((CHIPS - 2 * XH, ROWS, 128), jnp.float32)
    p_buf[0, NY:YP, :] = jnp.broadcast_to(offsets_ref[0, 1].astype(jnp.float32), (YP - NY, 128))
    pl.semaphore_wait(barrier, 2 + CHIPS - 1 + RING - 1)

    give_half = remote(term.at[pl.ds((1 - core) * SPOTS, SPOTS)], pair_in, pair_sems.at[0], pair_sems.at[1], partner)
    give_half.start()

    give_p = remote(p_buf, q_buf, p_sems.at[0], p_sems.at[1], left)
    give_p.start()

    @pl.loop(0, XH)
    def _(i):
        for half in range(2):
            x = i + XH * half
            for pair in (0, 2):
                g = jnp.where(low, plane(rows, x, pair), pltpu.roll(plane(rows, x, pair + 1), ZP, 1))
                g_buf[half, i, :, 64 * pair:64 * pair + 128] = g

    give_half.wait()
    half_sum[...] = term[pl.ds(core * SPOTS, SPOTS)] + pair_in[...]

    @pl.loop(1, SPOTS)
    def _(d):
        other, target = in_plane(d)
        remote(half_sum.at[other], plane_in.at[d - 1], plane_send, plane_recv, target).start()

    for load in fixed:
        load.wait()
    for t in range(3):
        forward_yz(t, p_buf, g_buf, d_own, y_ref, z_ref)

    @pl.loop(0, YP // 8)
    def _(yt):
        middle_x(yt, d_own, green_ref)

    @pl.loop(0, XH)
    def _(i):
        own_buf[i] = own_buf[i] * (jnp.exp(jnp.log(packed(i, NB + 1)) * (-2.0 / 3.0)) * -XC_COEF)

    give_p.wait_recv()

    for t in range(3):
        forward_yz(t, q_buf, g_buf, d_far, y_ref, z_ref)

    drain(half_sum.at[pl.ds(0, SPOTS - 1)], plane_send)
    drain(plane_in, plane_recv)
    part = half_sum[spot]
    for d in range(SPOTS - 1):
        part = part + plane_in[d]
    part_sum[...] = part

    @pl.loop(1, RING)
    def _(d):
        remote(part_sum, ring_in.at[d - 1], ring_send, ring_recv, in_ring(d)).start()

    @pl.loop(0, YP // 8)
    def _(yt):
        middle_x(yt, d_far, green_ref)

    lane_q = lax.broadcasted_iota(jnp.int32, (1, 256), 1) // ZP
    signs = jnp.zeros((1, 256), jnp.float32)
    for q in range(NB):
        signs = jnp.where(lane_q == q, signs_ref[q].astype(jnp.float32), signs)
    lane_q = lane_q.astype(jnp.float32)
    far_offset = q_buf[0, NY:NY + 1, :]
    far_w = signs * (lane_q >= jnp.concatenate([far_offset, far_offset], 1)).astype(jnp.float32)
    own_offset = jnp.broadcast_to(offsets_ref[0, 0].astype(jnp.float32), (1, 256))
    own_w = signs * (lane_q >= own_offset).astype(jnp.float32)

    def e_copy(t):
        planes = pl.ds(5 * t, 5)
        return remote(e_out.at[planes], e_in.at[planes], e_send.at[t], e_recv.at[t], right)

    for t in range(3):
        e_out[pl.ds(5 * t, 5)] = inverse_yz(t, g_buf, d_far, far_w, y_ref, z_ref)
        e_copy(t).start()

    drain(ring_in, ring_send)
    drain(ring_in, ring_recv)
    part = part_sum[...]
    for d in range(RING - 1):
        part = part + ring_in[d]
    part_all[...] = part
    mine = core * SPOTS + spot
    rho[mine] = part

    @pl.loop(1, SPOTS)
    def _(d):
        remote(part_all, rho.at[mine], all_send, all_recv, in_plane(d)[1]).start()

    for t in range(3):
        if t == 2:
            drain(rho.at[pl.ds(0, SPOTS - 1)], all_send)
            drain(rho.at[pl.ds(0, SPOTS - 1)], all_recv)
            our_half = rho.at[pl.ds(core * SPOTS, SPOTS)]
            swap = remote(our_half, our_half, swap_sems.at[0], swap_sems.at[1], partner)
            swap.start()
        planes = pl.ds(5 * t, 5)
        e_own[planes] = inverse_yz(t, g_buf, d_own, own_w, y_ref, z_ref)
    for t in range(3):
        e_copy(t).wait()

    swap.wait()

    for x in range(NX):
        i, half = x % XH, x // XH
        total = own_buf[i] * rho[pl.ds(2 * i, 2)].reshape(YP, 128) + (e_own[i] + e_in[i]) * -HYBRID
        lines_out[NY * x:NY * x + YP, :] = pltpu.roll(total, ZP, 1) if half else total
    join_rows(lines_out, out_ref)

    give_p.wait_send()


def per_device(ground_orbitals, occupation_signs, response_orbitals, window_offsets, ground_density):
    points = response_orbitals.shape[1]
    y_mats, z_mats, green = tables()
    vmem = pl.BlockSpec(memory_space=pltpu.VMEM)
    smem = pl.BlockSpec(memory_space=pltpu.SMEM)
    hbm = pl.BlockSpec(memory_space=pltpu.HBM)
    f32 = jnp.float32
    dma = pltpu.SemaphoreType.DMA
    grid_planes = pltpu.VMEM((XH, YP, 128), f32)
    wide_planes = pltpu.VMEM((2, XH, YP, 256), f32)

    def chunks(*count):
        return pltpu.VMEM((*count, ROWS, 128), f32)

    action = pl.pallas_call(
        kernel,
        out_shape=jax.ShapeDtypeStruct((6 * 8 * TILES, 128), f32),
        in_specs=[hbm, hbm, hbm, smem, smem, hbm, hbm, hbm],
        out_specs=vmem,
        scratch_shapes=[
            pltpu.VMEM(y_mats.shape, jnp.bfloat16), pltpu.VMEM(z_mats.shape, jnp.bfloat16), pltpu.VMEM(green.shape, f32),
            pltpu.VMEM((8, points), f32),
            pltpu.VMEM((8, 128), f32),
            pltpu.VMEM((8 * (NX * NY + YP - NY), 128), f32),
            wide_planes, grid_planes, grid_planes, grid_planes, wide_planes, wide_planes, grid_planes, grid_planes, grid_planes,
            pltpu.VMEM((6 * 256, 128), f32),
            chunks(CHIPS), chunks(SPOTS), chunks(SPOTS), chunks(SPOTS - 1), chunks(), chunks(RING - 1), chunks(), chunks(CHIPS),
            dma((PIECES + 1, 3)), dma((2,)), dma((3,)), dma((3,)), dma((2,)), dma, dma, dma, dma, dma, dma, dma((2,)),
        ],
        compiler_params=pltpu.CompilerParams(
            collective_id=0, has_side_effects=True, vmem_limit_bytes=57 << 20
        ),
    )(
        ground_orbitals, response_orbitals, ground_density,
        occupation_signs, window_offsets, y_mats, z_mats, green,
    )
    return action.reshape(1, -1)[:, :points]


def solution(mesh):
    placed = (P("orb", None), P("orb"), P(("orb", "grid"), None), P(("orb", "grid"), None), P())
    return jax.shard_map(
        per_device, mesh=mesh, in_specs=placed, out_specs=P(("orb", "grid"), None), check_vma=False
    )
```

```python
import math
import numpy as np
import ml_dtypes
import jax
import jax.numpy as jnp
from jax import lax
from jax.experimental import pallas as pl
from jax.experimental.pallas import tpu as pltpu
from jax.sharding import PartitionSpec as P

NX, NY, NZ = 30, 45, 60
NB = 4
YP, ZP = 48, 64
XH = NX // 2
XC_COEF = 0.3282
HYBRID = 0.25


def real_basis(n):
    j = np.arange(n)
    rows, waves = [np.ones(n) / math.sqrt(n)], [0]
    for m in range(1, (n - 1) // 2 + 1):
        rows += [math.sqrt(2 / n) * np.cos(2 * np.pi * m * j / n), math.sqrt(2 / n) * np.sin(2 * np.pi * m * j / n)]
        waves += [m, m]
    if n % 2 == 0:
        rows.append(np.cos(np.pi * j) / math.sqrt(n))
        waves.append(n // 2)
    return np.array(rows), np.array(waves)


def padded(matrix, size):
    return np.pad(matrix, ((0, size - matrix.shape[0]), (0, size - matrix.shape[1])))


def hi_lo(matrix):
    hi = matrix.astype(ml_dtypes.bfloat16)
    lo = (matrix - hi.astype(np.float64)).astype(ml_dtypes.bfloat16)
    return np.stack([hi, lo])


def tables():
    ty, my = real_basis(NY)
    tz, mz = real_basis(NZ)
    ty, tz = padded(ty, YP), padded(tz, ZP)
    wy = np.kron(np.eye(5), ty)
    wz = np.kron(np.eye(NB), tz.T)
    y_mats = np.stack([hi_lo(wy), hi_lo(wy.T)])
    z_mats = np.stack([hi_lo(wz), hi_lo(wz.T)])
    mx = np.arange(NX // 2 + 1)
    k2 = lambda m, n: (2 * np.pi * m / (0.5 * n)) ** 2
    squared = k2(mx, NX)[:, None, None] + k2(my, NY)[None, :, None] + k2(mz, NZ)[None, None, :]
    green = 4 * np.pi / (squared + 0.25)
    weight = np.where((mx == 0) | (mx == NX // 2), 1.0, 2.0) / NX
    green = green * weight[:, None, None]
    green = np.pad(green, ((0, 0), (0, YP - NY), (0, ZP - NZ)))
    green = np.concatenate([green, green], -1).astype(np.float32)
    return y_mats, z_mats, green


def split(x):
    hi = x.astype(jnp.bfloat16)
    return hi, (x - hi.astype(jnp.float32)).astype(jnp.bfloat16)


def dot(a, b):
    return lax.dot_general(a, b, (((1,), (0,)), ((), ())), preferred_element_type=jnp.float32)


def times_right(x, mat):
    hi, lo = split(x)
    return dot(hi, mat[0]) + dot(lo, mat[0]) + dot(hi, mat[1])


def times_left(mat, x):
    hi, lo = split(x)
    return dot(mat[0], hi) + dot(mat[0], lo) + dot(mat[1], hi)


C3, S3 = 0.5, math.sqrt(3) / 2
S5A, S5B, R5 = math.sin(2 * math.pi / 5), math.sin(4 * math.pi / 5), math.sqrt(5) / 4


def five_even(zero, one, two):
    total, apart = one + two, (one - two) * R5
    base = zero - total * 0.25
    return zero + total, base + apart, base - apart


def five_odd(one, two):
    return one * S5A + two * S5B, one * S5B - two * S5A


def five_waves(p):
    return five_even(p[0], p[1] + p[4], p[2] + p[3]) + five_odd(p[1] - p[4], p[2] - p[3])


def five_points(c):
    zero, one, two = five_even(*c[:3])
    up, down = five_odd(*c[3:])
    return [zero, one + up, two + down, two - down, one - up]


def wave_of(two, three, five):
    wave = next(m for m in range(NX) if (m % 2, m % 3, m % 5) == (two, three, five % 5))
    return min(wave, NX - wave)


def x_solve(p, green):
    grid = [[[p[(15 * a + 10 * b + 6 * c) % NX] for c in range(5)] for b in range(3)] for a in range(2)]
    back = []
    for two in range(2):
        rows = [[grid[0][b][c] - grid[1][b][c] if two else grid[0][b][c] + grid[1][b][c] for c in range(5)] for b in range(3)]
        both = [rows[1][c] + rows[2][c] for c in range(5)]
        flat = five_waves([rows[0][c] + both[c] for c in range(5)])
        cosine = five_waves([rows[0][c] - both[c] * C3 for c in range(5)])
        sine = five_waves([(rows[1][c] - rows[2][c]) * S3 for c in range(5)])
        k = lambda three, five: green[wave_of(two, three, five)]
        flat = [flat[0] * k(0, 0), flat[1] * k(0, 1), flat[2] * k(0, 2), flat[3] * k(0, 1), flat[4] * k(0, 2)]
        new_c, new_s = [cosine[0] * k(1, 0)] + [None] * 4, [sine[0] * k(1, 0)] + [None] * 4
        for five in (1, 2):
            cc, cs, sc, ss = cosine[five], cosine[five + 2], sine[five], sine[five + 2]
            x_up, x_down = (cc - ss) * k(1, five), (cc + ss) * k(1, -five)
            y_up, y_down = (sc + cs) * k(1, five), (sc - cs) * k(1, -five)
            new_c[five], new_s[five + 2] = x_up + x_down, x_down - x_up
            new_s[five], new_c[five + 2] = y_up + y_down, y_up - y_down
        flat, cosine, sine = five_points(flat), five_points(new_c), five_points(new_s)
        lines = [[flat[c] + cosine[c] for c in range(5)], [], []]
        for c in range(5):
            middle, side = flat[c] - cosine[c] * C3, sine[c] * S3
            lines[1].append(middle + side)
            lines[2].append(middle - side)
        back.append(lines)
    out = [None] * NX
    for a in range(2):
        for b in range(3):
            for c in range(5):
                plus, minus = back[0][b][c], back[1][b][c]
                out[(15 * a + 10 * b + 6 * c) % NX] = minus_or(plus, minus, a)
    return out


def minus_or(plus, minus, a):
    return plus - minus if a else plus + minus


def forward_yz(t, p_buf, g_buf, d_buf, y_ref, z_ref):
    planes = pl.ds(5 * t, 5)
    p = p_buf[planes].reshape(5 * YP, 128)
    turned = pltpu.roll(p, ZP, 1)
    low = lax.broadcasted_iota(jnp.int32, p.shape, 1) < ZP
    for half in range(2):
        both = jnp.where(low, p, turned) if half == 0 else jnp.where(low, turned, p)
        g = g_buf[half, planes].reshape(5 * YP, 256)
        s = times_right(jnp.concatenate([both, both], 1) * g, z_ref[0])
        d_buf[half, planes] = times_left(y_ref[0], s).reshape(5, YP, 256)


def middle_x(yt, d_buf, green_ref):
    rows = pl.ds(pl.multiple_of(8 * yt, 8), 8)
    green = [green_ref[m, rows, :] for m in range(16)]
    for lane in (0, 128):
        lanes = pl.ds(lane, 128)
        out = x_solve([d_buf[x // XH, x % XH, rows, lanes] for x in range(NX)], green)
        for x in range(NX):
            d_buf[x // XH, x % XH, rows, lanes] = out[x]


def inverse_yz(t, g_buf, d_buf, w, y_ref, z_ref):
    planes = pl.ds(5 * t, 5)
    sums = []
    for half in range(2):
        s = times_left(y_ref[1], d_buf[half, planes].reshape(5 * YP, 256))
        v = times_right(s, z_ref[1]) * (g_buf[half, planes].reshape(5 * YP, 256) * w)
        pair = v[:, :128] + v[:, 128:]
        sums.append(pair + pltpu.roll(pair, ZP, 1))
    low = lax.broadcasted_iota(jnp.int32, sums[0].shape, 1) < ZP
    return jnp.where(low, sums[0], sums[1]).reshape(5, YP, 128)


MESH = pl.DeviceIdType.MESH
SPOTS = 16
CHIPS = 32
RING = 8
ROWS = 24
WINDOW = 1920
TILES = 15
PIECES = 3
UNROLL = 7


def device(orb, grid):
    return {"orb": orb, "grid": grid}


def remote(src, dst, sends, arrivals, target):
    return pltpu.make_async_remote_copy(
        src_ref=src, dst_ref=dst, send_sem=sends, recv_sem=arrivals, device_id=target, device_id_type=MESH
    )


def drain(ref, sem):
    pltpu.make_async_copy(ref, ref, sem).wait()


def cut_rows(flat, last, rows, points, arrive, greetings):
    lane = lax.broadcasted_iota(jnp.int32, (8, 128), 1)

    def cut(base, count, tile):
        for r in range(count):
            j, off = divmod(NZ * r, 128)
            both = tile(j) if off <= 128 - NZ else jnp.where(lane < off, tile(j + 1), tile(j))
            rows[pl.ds(base + 8 * r, 8), :] = pltpu.roll(both, 128 - off, 1) if off else both

    whole = points // WINDOW
    tail = points - points // 128 * 128
    for piece in range(PIECES):
        arrive(piece)

        @pl.loop(0, whole // PIECES // UNROLL)
        def _(step):
            for u in range(UNROLL):
                k = piece * (whole // PIECES) + step * UNROLL + u
                greetings[piece](step * UNROLL + u)
                cut(
                    pl.multiple_of(k * 256, 256), 32,
                    lambda j: flat[:, pl.ds(pl.multiple_of(k * WINDOW + j * 128, 128), 128)],
                )

    end = whole * TILES
    last[...] = jnp.zeros((8, 128), jnp.float32)
    last[:, 0:tail] = flat[:, points - tail:points]
    cut(
        whole * 256, (points - whole * WINDOW) // NZ,
        lambda j: last[...] if end + j == points // 128 else flat[:, (end + j) * 128:(end + j + 1) * 128],
    )
    rows[8 * (NX * NY):8 * (NX * NY + YP - NY), :] = jnp.zeros((8 * (YP - NY), 128), jnp.float32)


def join_rows(lines, flat):
    lane = lax.broadcasted_iota(jnp.int32, (8, 128), 1)

    @pl.loop(0, flat.shape[0] // (8 * TILES))
    def _(m):
        turned = []
        for r in range(32):
            line = lines[pl.ds(256 * m + r, 8, stride=32), :]
            off = NZ * r % 128
            turned.append(pltpu.roll(line, off, 1) if off else line)
        for t in range(TILES):
            pieces = [r for r in range(32) if NZ * r < 128 * (t + 1) and NZ * (r + 1) > 128 * t]
            tile = turned[pieces[0]]
            for r in pieces[1:]:
                tile = jnp.where(lane >= NZ * r - 128 * t, turned[r], tile)
            flat[pl.ds(8 * TILES * m + t, 8, stride=TILES), :] = tile


def plane(rows, x, line):
    return rows[pl.ds(x * (8 * NY) + line, YP, stride=8), :]


def kernel(
    ground_ref, response_ref, density_ref, signs_ref, offsets_ref, y_hbm, z_hbm, green_hbm,
    out_ref,
    y_ref, z_ref, green_ref, flat, last, rows, g_buf, p_buf, q_buf, own_buf, d_own, d_far, e_out, e_in, e_own,
    lines_out, term, pair_in, half_sum, plane_in, part_sum, ring_in, part_all, rho,
    in_sems, p_sems, e_send, e_recv, pair_sems, plane_send, plane_recv, ring_send, ring_recv, all_send, all_recv, swap_sems,
):
    orb, grid = lax.axis_index("orb"), lax.axis_index("grid")
    core = lax.rem(orb, 2)
    z_lo = lax.rem(orb // 2, 2)
    spot = orb // 4
    level = grid * 2 + z_lo
    left = device(lax.rem(orb + 63, 64), grid)
    right = device(lax.rem(orb + 1, 64), grid)
    partner = device(orb + 1 - 2 * core, grid)

    points = flat.shape[1]
    cuts = [piece * (points // WINDOW // PIECES) * WINDOW for piece in range(PIECES)] + [points]
    lines = ((ground_ref, 0, NB), (response_ref, NB, 1), (density_ref, NB + 1, 1))
    loads = [
        [
            pltpu.make_async_copy(
                source.at[:, cuts[piece]:cuts[piece + 1]] if at < 2 else source.at[cuts[piece]:cuts[piece + 1]],
                flat.at[first:first + count, cuts[piece]:cuts[piece + 1]] if at < 2 else flat.at[first, cuts[piece]:cuts[piece + 1]],
                in_sems.at[piece, at],
            )
            for at, (source, first, count) in enumerate(lines)
        ]
        for piece in range(PIECES)
    ]
    fixed = (
        pltpu.make_async_copy(y_hbm, y_ref, in_sems.at[PIECES, 0]),
        pltpu.make_async_copy(z_hbm, z_ref, in_sems.at[PIECES, 1]),
        pltpu.make_async_copy(green_hbm, green_ref, in_sems.at[PIECES, 2]),
    )
    for load in sum(loads, []) + list(fixed):
        load.start()

    def in_plane(d):
        other = lax.rem(spot + d, SPOTS)
        return other, device(other * 4 + lax.rem(orb, 4), grid)

    def in_chips(d):
        other = lax.rem(spot * 2 + core + d, CHIPS)
        return device(other // 2 * 4 + z_lo * 2 + lax.rem(other, 2), grid)

    def in_ring(d):
        other = lax.rem(level + d, RING)
        return device(spot * 4 + lax.rem(other, 2) * 2 + core, other // 2)

    barrier = pltpu.get_barrier_semaphore()

    def greet(target):
        pl.semaphore_signal(barrier, inc=1, device_id=target, device_id_type=MESH)

    for target in (left, right):
        greet(target)

    @pl.loop(1, CHIPS - 28)
    def _(d):
        greet(in_chips(d))

    @pl.loop(1, RING)
    def _(d):
        greet(in_ring(d))

    def arrive(piece):
        for load in loads[piece]:
            load.wait()

    greetings = (
        lambda at: greet(in_chips(CHIPS - 28 + at)),
        lambda at: greet(in_chips(CHIPS - 14 + at)),
        lambda at: None,
    )
    cut_rows(flat, last, rows, points, arrive, greetings)

    low = lax.broadcasted_iota(jnp.int32, (YP, 128), 1) < ZP
    own_sign = signs_ref[grid].astype(jnp.float32)

    def packed(i, line):
        return jnp.where(low, plane(rows, i, line), pltpu.roll(plane(rows, i + XH, line), ZP, 1))

    @pl.loop(0, XH)
    def _(i):
        p, own = packed(i, NB), packed(i, grid)
        p_buf[i] = p
        own_buf[i] = own
        term[pl.ds(2 * i, 2)] = (own * own_sign * p).reshape(2, ROWS, 128)

    term[2 * XH:CHIPS] = jnp.zeros((CHIPS - 2 * XH, ROWS, 128), jnp.float32)
    p_buf[0, NY:YP, :] = jnp.broadcast_to(offsets_ref[0, 1].astype(jnp.float32), (YP - NY, 128))
    pl.semaphore_wait(barrier, 2 + CHIPS - 1 + RING - 1)

    give_half = remote(term.at[pl.ds((1 - core) * SPOTS, SPOTS)], pair_in, pair_sems.at[0], pair_sems.at[1], partner)
    give_half.start()

    give_p = remote(p_buf, q_buf, p_sems.at[0], p_sems.at[1], left)
    give_p.start()

    @pl.loop(0, XH)
    def _(i):
        for half in range(2):
            x = i + XH * half
            for pair in (0, 2):
                g = jnp.where(low, plane(rows, x, pair), pltpu.roll(plane(rows, x, pair + 1), ZP, 1))
                g_buf[half, i, :, 64 * pair:64 * pair + 128] = g

    give_half.wait()
    half_sum[...] = term[pl.ds(core * SPOTS, SPOTS)] + pair_in[...]

    @pl.loop(1, SPOTS)
    def _(d):
        other, target = in_plane(d)
        remote(half_sum.at[other], plane_in.at[d - 1], plane_send, plane_recv, target).start()

    for load in fixed:
        load.wait()
    for t in range(3):
        forward_yz(t, p_buf, g_buf, d_own, y_ref, z_ref)

    @pl.loop(0, YP // 8)
    def _(yt):
        middle_x(yt, d_own, green_ref)

    @pl.loop(0, XH)
    def _(i):
        own_buf[i] = own_buf[i] * (jnp.exp(jnp.log(packed(i, NB + 1)) * (-2.0 / 3.0)) * -XC_COEF)

    give_p.wait_recv()

    for t in range(3):
        forward_yz(t, q_buf, g_buf, d_far, y_ref, z_ref)

    drain(half_sum.at[pl.ds(0, SPOTS - 1)], plane_send)
    drain(plane_in, plane_recv)
    part = half_sum[spot]
    for d in range(SPOTS - 1):
        part = part + plane_in[d]
    part_sum[...] = part

    @pl.loop(1, RING)
    def _(d):
        remote(part_sum, ring_in.at[d - 1], ring_send, ring_recv, in_ring(d)).start()

    @pl.loop(0, YP // 8)
    def _(yt):
        middle_x(yt, d_far, green_ref)

    lane_q = lax.broadcasted_iota(jnp.int32, (1, 256), 1) // ZP
    signs = jnp.zeros((1, 256), jnp.float32)
    for q in range(NB):
        signs = jnp.where(lane_q == q, signs_ref[q].astype(jnp.float32), signs)
    lane_q = lane_q.astype(jnp.float32)
    far_offset = q_buf[0, NY:NY + 1, :]
    far_w = signs * (lane_q >= jnp.concatenate([far_offset, far_offset], 1)).astype(jnp.float32)
    own_offset = jnp.broadcast_to(offsets_ref[0, 0].astype(jnp.float32), (1, 256))
    own_w = signs * (lane_q >= own_offset).astype(jnp.float32)

    def e_copy(t):
        planes = pl.ds(5 * t, 5)
        return remote(e_out.at[planes], e_in.at[planes], e_send.at[t], e_recv.at[t], right)

    for t in range(3):
        e_out[pl.ds(5 * t, 5)] = inverse_yz(t, g_buf, d_far, far_w, y_ref, z_ref)
        e_copy(t).start()

    drain(ring_in, ring_send)
    drain(ring_in, ring_recv)
    part = part_sum[...]
    for d in range(RING - 1):
        part = part + ring_in[d]
    part_all[...] = part
    mine = core * SPOTS + spot
    rho[mine] = part

    @pl.loop(1, SPOTS)
    def _(d):
        remote(part_all, rho.at[mine], all_send, all_recv, in_plane(d)[1]).start()

    for t in range(3):
        if t == 2:
            drain(rho.at[pl.ds(0, SPOTS - 1)], all_send)
            drain(rho.at[pl.ds(0, SPOTS - 1)], all_recv)
            our_half = rho.at[pl.ds(core * SPOTS, SPOTS)]
            swap = remote(our_half, our_half, swap_sems.at[0], swap_sems.at[1], partner)
            swap.start()
        planes = pl.ds(5 * t, 5)
        e_own[planes] = inverse_yz(t, g_buf, d_own, own_w, y_ref, z_ref)
    for t in range(3):
        e_copy(t).wait()

    swap.wait()

    for x in range(NX):
        i, half = x % XH, x // XH
        total = own_buf[i] * rho[pl.ds(2 * i, 2)].reshape(YP, 128) + (e_own[i] + e_in[i]) * -HYBRID
        lines_out[NY * x:NY * x + YP, :] = pltpu.roll(total, ZP, 1) if half else total
    join_rows(lines_out, out_ref)

    give_p.wait_send()


def per_device(ground_orbitals, occupation_signs, response_orbitals, window_offsets, ground_density):
    points = response_orbitals.shape[1]
    y_mats, z_mats, green = tables()
    vmem = pl.BlockSpec(memory_space=pltpu.VMEM)
    smem = pl.BlockSpec(memory_space=pltpu.SMEM)
    hbm = pl.BlockSpec(memory_space=pltpu.HBM)
    f32 = jnp.float32
    dma = pltpu.SemaphoreType.DMA
    grid_planes = pltpu.VMEM((XH, YP, 128), f32)
    wide_planes = pltpu.VMEM((2, XH, YP, 256), f32)

    def chunks(*count):
        return pltpu.VMEM((*count, ROWS, 128), f32)

    action = pl.pallas_call(
        kernel,
        out_shape=jax.ShapeDtypeStruct((6 * 8 * TILES, 128), f32),
        in_specs=[hbm, hbm, hbm, smem, smem, hbm, hbm, hbm],
        out_specs=vmem,
        scratch_shapes=[
            pltpu.VMEM(y_mats.shape, jnp.bfloat16), pltpu.VMEM(z_mats.shape, jnp.bfloat16), pltpu.VMEM(green.shape, f32),
            pltpu.VMEM((8, points), f32),
            pltpu.VMEM((8, 128), f32),
            pltpu.VMEM((8 * (NX * NY + YP - NY), 128), f32),
            wide_planes, grid_planes, grid_planes, grid_planes, wide_planes, wide_planes, grid_planes, grid_planes, grid_planes,
            pltpu.VMEM((6 * 256, 128), f32),
            chunks(CHIPS), chunks(SPOTS), chunks(SPOTS), chunks(SPOTS - 1), chunks(), chunks(RING - 1), chunks(), chunks(CHIPS),
            dma((PIECES + 1, 3)), dma((2,)), dma((3,)), dma((3,)), dma((2,)), dma, dma, dma, dma, dma, dma, dma((2,)),
        ],
        compiler_params=pltpu.CompilerParams(
            collective_id=0, has_side_effects=True, vmem_limit_bytes=40 << 20
        ),
    )(
        *(pltpu.with_memory_space_constraint(x, pltpu.HBM) for x in (ground_orbitals, response_orbitals, ground_density)),
        *(pltpu.with_memory_space_constraint(x, pltpu.HBM) for x in (occupation_signs, window_offsets)),
        *(pltpu.with_memory_space_constraint(jnp.asarray(x), pltpu.HBM) for x in (y_mats, z_mats, green)),
    )
    return action.reshape(1, -1)[:, :points]


def solution(mesh):
    placed = (P("orb", None), P("orb"), P(("orb", "grid"), None), P(("orb", "grid"), None), P())
    return jax.shard_map(
        per_device, mesh=mesh, in_specs=placed, out_specs=P(("orb", "grid"), None), check_vma=False
    )
```

```python
import math
import numpy as np
import ml_dtypes
import jax
import jax.numpy as jnp
from jax import lax
from jax.experimental import pallas as pl
from jax.experimental.pallas import tpu as pltpu
from jax.sharding import PartitionSpec as P

NX, NY, NZ = 30, 45, 60
NB = 4
YP, ZP = 48, 64
XH = NX // 2
XC_COEF = 0.3282
HYBRID = 0.25


def real_basis(n):
    j = np.arange(n)
    rows, waves = [np.ones(n) / math.sqrt(n)], [0]
    for m in range(1, (n - 1) // 2 + 1):
        rows += [math.sqrt(2 / n) * np.cos(2 * np.pi * m * j / n), math.sqrt(2 / n) * np.sin(2 * np.pi * m * j / n)]
        waves += [m, m]
    if n % 2 == 0:
        rows.append(np.cos(np.pi * j) / math.sqrt(n))
        waves.append(n // 2)
    return np.array(rows), np.array(waves)


def padded(matrix, size):
    return np.pad(matrix, ((0, size - matrix.shape[0]), (0, size - matrix.shape[1])))


def hi_lo(matrix):
    hi = matrix.astype(ml_dtypes.bfloat16)
    lo = (matrix - hi.astype(np.float64)).astype(ml_dtypes.bfloat16)
    return np.stack([hi, lo])


def tables():
    ty, my = real_basis(NY)
    tz, mz = real_basis(NZ)
    ty, tz = padded(ty, YP), padded(tz, ZP)
    wy = np.kron(np.eye(5), ty)
    wz = np.kron(np.eye(NB), tz.T)
    y_mats = np.stack([hi_lo(wy), hi_lo(wy.T)])
    z_mats = np.stack([hi_lo(wz), hi_lo(wz.T)])
    mx = np.arange(NX // 2 + 1)
    k2 = lambda m, n: (2 * np.pi * m / (0.5 * n)) ** 2
    squared = k2(mx, NX)[:, None, None] + k2(my, NY)[None, :, None] + k2(mz, NZ)[None, None, :]
    green = 4 * np.pi / (squared + 0.25)
    weight = np.where((mx == 0) | (mx == NX // 2), 1.0, 2.0) / NX
    green = green * weight[:, None, None]
    green = np.pad(green, ((0, 0), (0, YP - NY), (0, ZP - NZ)))
    green = np.concatenate([green, green], -1).astype(np.float32)
    return y_mats, z_mats, green


def split(x):
    hi = x.astype(jnp.bfloat16)
    return hi, (x - hi.astype(jnp.float32)).astype(jnp.bfloat16)


def dot(a, b):
    return lax.dot_general(a, b, (((1,), (0,)), ((), ())), preferred_element_type=jnp.float32)


def times_right(x, mat):
    hi, lo = split(x)
    return dot(hi, mat[0]) + dot(lo, mat[0]) + dot(hi, mat[1])


def times_left(mat, x):
    hi, lo = split(x)
    return dot(mat[0], hi) + dot(mat[0], lo) + dot(mat[1], hi)


C3, S3 = 0.5, math.sqrt(3) / 2
S5A, S5B, R5 = math.sin(2 * math.pi / 5), math.sin(4 * math.pi / 5), math.sqrt(5) / 4


def five_even(zero, one, two):
    total, apart = one + two, (one - two) * R5
    base = zero - total * 0.25
    return zero + total, base + apart, base - apart


def five_odd(one, two):
    return one * S5A + two * S5B, one * S5B - two * S5A


def five_waves(p):
    return five_even(p[0], p[1] + p[4], p[2] + p[3]) + five_odd(p[1] - p[4], p[2] - p[3])


def five_points(c):
    zero, one, two = five_even(*c[:3])
    up, down = five_odd(*c[3:])
    return [zero, one + up, two + down, two - down, one - up]


def wave_of(two, three, five):
    wave = next(m for m in range(NX) if (m % 2, m % 3, m % 5) == (two, three, five % 5))
    return min(wave, NX - wave)


def x_solve(p, green):
    grid = [[[p[(15 * a + 10 * b + 6 * c) % NX] for c in range(5)] for b in range(3)] for a in range(2)]
    back = []
    for two in range(2):
        rows = [[grid[0][b][c] - grid[1][b][c] if two else grid[0][b][c] + grid[1][b][c] for c in range(5)] for b in range(3)]
        both = [rows[1][c] + rows[2][c] for c in range(5)]
        flat = five_waves([rows[0][c] + both[c] for c in range(5)])
        cosine = five_waves([rows[0][c] - both[c] * C3 for c in range(5)])
        sine = five_waves([(rows[1][c] - rows[2][c]) * S3 for c in range(5)])
        k = lambda three, five: green[wave_of(two, three, five)]
        flat = [flat[0] * k(0, 0), flat[1] * k(0, 1), flat[2] * k(0, 2), flat[3] * k(0, 1), flat[4] * k(0, 2)]
        new_c, new_s = [cosine[0] * k(1, 0)] + [None] * 4, [sine[0] * k(1, 0)] + [None] * 4
        for five in (1, 2):
            cc, cs, sc, ss = cosine[five], cosine[five + 2], sine[five], sine[five + 2]
            x_up, x_down = (cc - ss) * k(1, five), (cc + ss) * k(1, -five)
            y_up, y_down = (sc + cs) * k(1, five), (sc - cs) * k(1, -five)
            new_c[five], new_s[five + 2] = x_up + x_down, x_down - x_up
            new_s[five], new_c[five + 2] = y_up + y_down, y_up - y_down
        flat, cosine, sine = five_points(flat), five_points(new_c), five_points(new_s)
        lines = [[flat[c] + cosine[c] for c in range(5)], [], []]
        for c in range(5):
            middle, side = flat[c] - cosine[c] * C3, sine[c] * S3
            lines[1].append(middle + side)
            lines[2].append(middle - side)
        back.append(lines)
    out = [None] * NX
    for a in range(2):
        for b in range(3):
            for c in range(5):
                plus, minus = back[0][b][c], back[1][b][c]
                out[(15 * a + 10 * b + 6 * c) % NX] = minus_or(plus, minus, a)
    return out


def minus_or(plus, minus, a):
    return plus - minus if a else plus + minus


def forward_yz(t, p_buf, g_buf, d_buf, y_ref, z_ref):
    planes = pl.ds(5 * t, 5)
    p = p_buf[planes].reshape(5 * YP, 128)
    turned = pltpu.roll(p, ZP, 1)
    low = lax.broadcasted_iota(jnp.int32, p.shape, 1) < ZP
    for half in range(2):
        both = jnp.where(low, p, turned) if half == 0 else jnp.where(low, turned, p)
        g = g_buf[half, planes].reshape(5 * YP, 256)
        s = times_right(jnp.concatenate([both, both], 1) * g, z_ref[0])
        d_buf[half, planes] = times_left(y_ref[0], s).reshape(5, YP, 256)


def middle_x(yt, d_buf, green_ref):
    rows = pl.ds(pl.multiple_of(8 * yt, 8), 8)
    green = [green_ref[m, rows, :] for m in range(16)]
    for lane in (0, 128):
        lanes = pl.ds(lane, 128)
        out = x_solve([d_buf[x // XH, x % XH, rows, lanes] for x in range(NX)], green)
        for x in range(NX):
            d_buf[x // XH, x % XH, rows, lanes] = out[x]


def inverse_yz(t, g_buf, d_buf, w, y_ref, z_ref):
    planes = pl.ds(5 * t, 5)
    sums = []
    for half in range(2):
        s = times_left(y_ref[1], d_buf[half, planes].reshape(5 * YP, 256))
        v = times_right(s, z_ref[1]) * (g_buf[half, planes].reshape(5 * YP, 256) * w)
        pair = v[:, :128] + v[:, 128:]
        sums.append(pair + pltpu.roll(pair, ZP, 1))
    low = lax.broadcasted_iota(jnp.int32, sums[0].shape, 1) < ZP
    return jnp.where(low, sums[0], sums[1]).reshape(5, YP, 128)


MESH = pl.DeviceIdType.MESH
SPOTS = 16
CHIPS = 32
RING = 8
ROWS = 24
WINDOW = 1920
TILES = 15
PIECES = 3
UNROLL = 7


def device(orb, grid):
    return {"orb": orb, "grid": grid}


def remote(src, dst, sends, arrivals, target):
    return pltpu.make_async_remote_copy(
        src_ref=src, dst_ref=dst, send_sem=sends, recv_sem=arrivals, device_id=target, device_id_type=MESH
    )


def drain(ref, sem):
    pltpu.make_async_copy(ref, ref, sem).wait()


def cut_rows(flat, last, rows, points, arrive, greetings):
    lane = lax.broadcasted_iota(jnp.int32, (8, 128), 1)

    def cut(base, count, tile):
        for r in range(count):
            j, off = divmod(NZ * r, 128)
            both = tile(j) if off <= 128 - NZ else jnp.where(lane < off, tile(j + 1), tile(j))
            rows[pl.ds(base + 8 * r, 8), :] = pltpu.roll(both, 128 - off, 1) if off else both

    whole = points // WINDOW
    tail = points - points // 128 * 128
    for piece in range(PIECES):
        arrive(piece)

        @pl.loop(0, whole // PIECES // UNROLL)
        def _(step):
            for u in range(UNROLL):
                k = piece * (whole // PIECES) + step * UNROLL + u
                greetings[piece](step * UNROLL + u)
                cut(
                    pl.multiple_of(k * 256, 256), 32,
                    lambda j: flat[:, pl.ds(pl.multiple_of(k * WINDOW + j * 128, 128), 128)],
                )

    end = whole * TILES
    last[...] = jnp.zeros((8, 128), jnp.float32)
    last[:, 0:tail] = flat[:, points - tail:points]
    cut(
        whole * 256, (points - whole * WINDOW) // NZ,
        lambda j: last[...] if end + j == points // 128 else flat[:, (end + j) * 128:(end + j + 1) * 128],
    )
    rows[8 * (NX * NY):8 * (NX * NY + YP - NY), :] = jnp.zeros((8 * (YP - NY), 128), jnp.float32)


def join_rows(lines, flat):
    lane = lax.broadcasted_iota(jnp.int32, (8, 128), 1)

    points = flat.shape[1]

    def join(m, whole):
        turned = []
        for r in range(32):
            line = lines[pl.ds(256 * m + r, 8, stride=32), :]
            off = NZ * r % 128
            turned.append(pltpu.roll(line, off, 1) if off else line)
        for t in range(TILES):
            pieces = [r for r in range(32) if NZ * r < 128 * (t + 1) and NZ * (r + 1) > 128 * t]
            tile = turned[pieces[0]]
            for r in pieces[1:]:
                tile = jnp.where(lane >= NZ * r - 128 * t, turned[r], tile)
            for group in range(8):
                at = (8 * m + group) * WINDOW + 128 * t
                if whole:
                    flat[:, pl.ds(pl.multiple_of(at, 128), 128)] = tile[group:group + 1]
                elif at < points:
                    width = min(128, points - at)
                    flat[:, at:at + width] = tile[group:group + 1, :width]

    full = points // (8 * WINDOW)

    @pl.loop(0, full)
    def _(m):
        join(m, True)

    join(full, False)


def plane(rows, x, line):
    return rows[pl.ds(x * (8 * NY) + line, YP, stride=8), :]


def kernel(
    ground_ref, response_ref, density_ref, signs_ref, offsets_ref, y_hbm, z_hbm, green_hbm,
    out_ref,
    y_ref, z_ref, green_ref, flat, last, rows, g_buf, p_buf, q_buf, own_buf, d_own, d_far, e_out, e_in, e_own,
    lines_out, term, pair_in, half_sum, plane_in, part_sum, ring_in, part_all, rho,
    in_sems, p_sems, e_send, e_recv, pair_sems, plane_send, plane_recv, ring_send, ring_recv, all_send, all_recv, swap_sems,
):
    orb, grid = lax.axis_index("orb"), lax.axis_index("grid")
    core = lax.rem(orb, 2)
    z_lo = lax.rem(orb // 2, 2)
    spot = orb // 4
    level = grid * 2 + z_lo
    left = device(lax.rem(orb + 63, 64), grid)
    right = device(lax.rem(orb + 1, 64), grid)
    partner = device(orb + 1 - 2 * core, grid)

    points = flat.shape[1]
    cuts = [piece * (points // WINDOW // PIECES) * WINDOW for piece in range(PIECES)] + [points]
    lines = ((ground_ref, 0, NB), (response_ref, NB, 1), (density_ref, NB + 1, 1))
    loads = [
        [
            pltpu.make_async_copy(
                source.at[:, cuts[piece]:cuts[piece + 1]] if at < 2 else source.at[cuts[piece]:cuts[piece + 1]],
                flat.at[first:first + count, cuts[piece]:cuts[piece + 1]] if at < 2 else flat.at[first, cuts[piece]:cuts[piece + 1]],
                in_sems.at[piece, at],
            )
            for at, (source, first, count) in enumerate(lines)
        ]
        for piece in range(PIECES)
    ]
    fixed = (
        pltpu.make_async_copy(y_hbm, y_ref, in_sems.at[PIECES, 0]),
        pltpu.make_async_copy(z_hbm, z_ref, in_sems.at[PIECES, 1]),
        pltpu.make_async_copy(green_hbm, green_ref, in_sems.at[PIECES, 2]),
    )
    for load in sum(loads, []) + list(fixed):
        load.start()

    def in_plane(d):
        other = lax.rem(spot + d, SPOTS)
        return other, device(other * 4 + lax.rem(orb, 4), grid)

    def in_chips(d):
        other = lax.rem(spot * 2 + core + d, CHIPS)
        return device(other // 2 * 4 + z_lo * 2 + lax.rem(other, 2), grid)

    def in_ring(d):
        other = lax.rem(level + d, RING)
        return device(spot * 4 + lax.rem(other, 2) * 2 + core, other // 2)

    barrier = pltpu.get_barrier_semaphore()

    def greet(target):
        pl.semaphore_signal(barrier, inc=1, device_id=target, device_id_type=MESH)

    for target in (left, right):
        greet(target)

    @pl.loop(1, CHIPS - 28)
    def _(d):
        greet(in_chips(d))

    @pl.loop(1, RING)
    def _(d):
        greet(in_ring(d))

    def arrive(piece):
        for load in loads[piece]:
            load.wait()

    greetings = (
        lambda at: greet(in_chips(CHIPS - 28 + at)),
        lambda at: greet(in_chips(CHIPS - 14 + at)),
        lambda at: None,
    )
    cut_rows(flat, last, rows, points, arrive, greetings)

    low = lax.broadcasted_iota(jnp.int32, (YP, 128), 1) < ZP
    own_sign = signs_ref[grid].astype(jnp.float32)

    def packed(i, line):
        return jnp.where(low, plane(rows, i, line), pltpu.roll(plane(rows, i + XH, line), ZP, 1))

    @pl.loop(0, XH)
    def _(i):
        p, own = packed(i, NB), packed(i, grid)
        p_buf[i] = p
        own_buf[i] = own
        term[pl.ds(2 * i, 2)] = (own * own_sign * p).reshape(2, ROWS, 128)

    term[2 * XH:CHIPS] = jnp.zeros((CHIPS - 2 * XH, ROWS, 128), jnp.float32)
    p_buf[0, NY:YP, :] = jnp.broadcast_to(offsets_ref[0, 1].astype(jnp.float32), (YP - NY, 128))
    pl.semaphore_wait(barrier, 2 + CHIPS - 1 + RING - 1)

    give_half = remote(term.at[pl.ds((1 - core) * SPOTS, SPOTS)], pair_in, pair_sems.at[0], pair_sems.at[1], partner)
    give_half.start()

    give_p = remote(p_buf, q_buf, p_sems.at[0], p_sems.at[1], left)
    give_p.start()

    @pl.loop(0, XH)
    def _(i):
        for half in range(2):
            x = i + XH * half
            for pair in (0, 2):
                g = jnp.where(low, plane(rows, x, pair), pltpu.roll(plane(rows, x, pair + 1), ZP, 1))
                g_buf[half, i, :, 64 * pair:64 * pair + 128] = g

    give_half.wait()
    half_sum[...] = term[pl.ds(core * SPOTS, SPOTS)] + pair_in[...]

    @pl.loop(1, SPOTS)
    def _(d):
        other, target = in_plane(d)
        remote(half_sum.at[other], plane_in.at[d - 1], plane_send, plane_recv, target).start()

    for load in fixed:
        load.wait()
    for t in range(3):
        forward_yz(t, p_buf, g_buf, d_own, y_ref, z_ref)

    @pl.loop(0, YP // 8)
    def _(yt):
        middle_x(yt, d_own, green_ref)

    @pl.loop(0, XH)
    def _(i):
        own_buf[i] = own_buf[i] * (jnp.exp(jnp.log(packed(i, NB + 1)) * (-2.0 / 3.0)) * -XC_COEF)

    give_p.wait_recv()

    for t in range(3):
        forward_yz(t, q_buf, g_buf, d_far, y_ref, z_ref)

    drain(half_sum.at[pl.ds(0, SPOTS - 1)], plane_send)
    drain(plane_in, plane_recv)
    part = half_sum[spot]
    for d in range(SPOTS - 1):
        part = part + plane_in[d]
    part_sum[...] = part

    @pl.loop(1, RING)
    def _(d):
        remote(part_sum, ring_in.at[d - 1], ring_send, ring_recv, in_ring(d)).start()

    @pl.loop(0, YP // 8)
    def _(yt):
        middle_x(yt, d_far, green_ref)

    lane_q = lax.broadcasted_iota(jnp.int32, (1, 256), 1) // ZP
    signs = jnp.zeros((1, 256), jnp.float32)
    for q in range(NB):
        signs = jnp.where(lane_q == q, signs_ref[q].astype(jnp.float32), signs)
    lane_q = lane_q.astype(jnp.float32)
    far_offset = q_buf[0, NY:NY + 1, :]
    far_w = signs * (lane_q >= jnp.concatenate([far_offset, far_offset], 1)).astype(jnp.float32)
    own_offset = jnp.broadcast_to(offsets_ref[0, 0].astype(jnp.float32), (1, 256))
    own_w = signs * (lane_q >= own_offset).astype(jnp.float32)

    def e_copy(t):
        planes = pl.ds(5 * t, 5)
        return remote(e_out.at[planes], e_in.at[planes], e_send.at[t], e_recv.at[t], right)

    for t in range(3):
        e_out[pl.ds(5 * t, 5)] = inverse_yz(t, g_buf, d_far, far_w, y_ref, z_ref)
        e_copy(t).start()

    drain(ring_in, ring_send)
    drain(ring_in, ring_recv)
    part = part_sum[...]
    for d in range(RING - 1):
        part = part + ring_in[d]
    part_all[...] = part
    mine = core * SPOTS + spot
    rho[mine] = part

    @pl.loop(1, SPOTS)
    def _(d):
        remote(part_all, rho.at[mine], all_send, all_recv, in_plane(d)[1]).start()

    for t in range(3):
        if t == 2:
            drain(rho.at[pl.ds(0, SPOTS - 1)], all_send)
            drain(rho.at[pl.ds(0, SPOTS - 1)], all_recv)
            our_half = rho.at[pl.ds(core * SPOTS, SPOTS)]
            swap = remote(our_half, our_half, swap_sems.at[0], swap_sems.at[1], partner)
            swap.start()
        planes = pl.ds(5 * t, 5)
        e_own[planes] = inverse_yz(t, g_buf, d_own, own_w, y_ref, z_ref)
    for t in range(3):
        e_copy(t).wait()

    swap.wait()

    for x in range(NX):
        i, half = x % XH, x // XH
        total = own_buf[i] * rho[pl.ds(2 * i, 2)].reshape(YP, 128) + (e_own[i] + e_in[i]) * -HYBRID
        lines_out[NY * x:NY * x + YP, :] = pltpu.roll(total, ZP, 1) if half else total
    join_rows(lines_out, out_ref)

    give_p.wait_send()


def per_device(ground_orbitals, occupation_signs, response_orbitals, window_offsets, ground_density):
    points = response_orbitals.shape[1]
    y_mats, z_mats, green = tables()
    vmem = pl.BlockSpec(memory_space=pltpu.VMEM)
    smem = pl.BlockSpec(memory_space=pltpu.SMEM)
    hbm = pl.BlockSpec(memory_space=pltpu.HBM)
    f32 = jnp.float32
    dma = pltpu.SemaphoreType.DMA
    grid_planes = pltpu.VMEM((XH, YP, 128), f32)
    wide_planes = pltpu.VMEM((2, XH, YP, 256), f32)

    def chunks(*count):
        return pltpu.VMEM((*count, ROWS, 128), f32)

    action = pl.pallas_call(
        kernel,
        out_shape=jax.ShapeDtypeStruct((1, points), f32),
        in_specs=[hbm, hbm, hbm, smem, smem, hbm, hbm, hbm],
        out_specs=vmem,
        scratch_shapes=[
            pltpu.VMEM(y_mats.shape, jnp.bfloat16), pltpu.VMEM(z_mats.shape, jnp.bfloat16), pltpu.VMEM(green.shape, f32),
            pltpu.VMEM((8, points), f32),
            pltpu.VMEM((8, 128), f32),
            pltpu.VMEM((8 * (NX * NY + YP - NY), 128), f32),
            wide_planes, grid_planes, grid_planes, grid_planes, wide_planes, wide_planes, grid_planes, grid_planes, grid_planes,
            pltpu.VMEM((6 * 256, 128), f32),
            chunks(CHIPS), chunks(SPOTS), chunks(SPOTS), chunks(SPOTS - 1), chunks(), chunks(RING - 1), chunks(), chunks(CHIPS),
            dma((PIECES + 1, 3)), dma((2,)), dma((3,)), dma((3,)), dma((2,)), dma, dma, dma, dma, dma, dma, dma((2,)),
        ],
        compiler_params=pltpu.CompilerParams(
            collective_id=0, has_side_effects=True, vmem_limit_bytes=40 << 20
        ),
    )(
        *(pltpu.with_memory_space_constraint(x, pltpu.HBM) for x in (ground_orbitals, response_orbitals, ground_density)),
        *(pltpu.with_memory_space_constraint(x, pltpu.HBM) for x in (occupation_signs, window_offsets)),
        *(pltpu.with_memory_space_constraint(jnp.asarray(x), pltpu.HBM) for x in (y_mats, z_mats, green)),
    )
    return action


def solution(mesh):
    placed = (P("orb", None), P("orb"), P(("orb", "grid"), None), P(("orb", "grid"), None), P())
    return jax.shard_map(
        per_device, mesh=mesh, in_specs=placed, out_specs=P(("orb", "grid"), None), check_vma=False
    )
```
